32 devices in a mesh: span: 8 (over z, x), wall: 4 (over y, core).
Axes of the slice: x: 2, y: 2, z: 4, core: 2. Of those that a mesh axis runs over, the one named last changes fastest.
Arguments:
- forcing: float32 [768, 16384], P('wall', 'span'), may hold values from -6 to 6
- start: float32 [768, 16384], P('wall', 'span'), may hold values from -2 to 2
- wall_even: float32 [384, 384], replicated, may hold values from -0.3125 to 0.3125
- wall_odd: float32 [384, 384], replicated, may hold values from -0.3125 to 0.3125
- diag_shift: float32 [768, 512], P('wall', 'span'), may hold values from 0.5 to 2
- band_coef: float32 [8, 768, 512], P(None, 'wall', 'span'), may hold values from -2 to 2
- offsets: int32 [8], replicated, may hold values from -128 to 128, as said below
- pattern: int32 [8, 512], P(None, 'span'), may hold values 0 or 1
- block_inv: float32 [768, 192], P('wall'), may hold values from -0.109375 to 0.109375
Outputs:
- solution: float32 [768, 16384], P('wall', 'span')
- residual: float32 [768, 16384], P('wall', 'span')
The draws below stay inside these ranges and needn't reach their ends.
Inputs may be any that keep to these rules, and one draw needn't show every extreme that they name: `offsets`: every offset lies within 128 spanwise points; in every draw one band has offset 2 * 64 and one has offset -128.
All inputs are finite; a program needn't handle non-finite values. No bound on the sum of `pattern` on one device may be relied on, other than what follows from the above.
Results may differ from the reference program's by a relative error of at most 0.0001.
Values sent between devices are 32-bit elements; how exact they have to be, the bound alone decides.
No kernel may reach another device: no remote copies, remote signals or barrier semaphores. Data moves between devices by JAX's collectives and lax.ppermute only.
A program may use at most 128 MiB of HBM per device.

```python
import jax
import jax.numpy as jnp
from jax import lax

NY = 768
Z_DEV = 64
COLS = 32
BANDS = 8
SWEEPS = 2
HALF_NY = 384
WALL_ROWS = 192
NZ = 512
N_WALL = 4


def draw_offsets(key, part):
    first, second, third, fourth = jax.random.split(jax.random.fold_in(key, 17), 4)
    reach = 2 * Z_DEV
    values = jax.random.randint(first, (BANDS,), -reach, reach + 1)
    order = jax.random.permutation(second, BANDS)
    near_up = jax.random.randint(third, (), 1, reach)
    near_down = -jax.random.randint(fourth, (), 1, reach)
    values = values.at[order[0]].set(reach)
    values = values.at[order[1]].set(-reach)
    values = values.at[order[2]].set(near_up)
    values = values.at[order[3]].set(near_down)
    return values.astype(jnp.int32)


def set_ends(drawn, own_key, low, top_value):
    extent = drawn.shape
    index_at = [jax.random.randint(jax.random.fold_in(own_key, axis), (), 0, extent[axis]) for axis in range(len(extent))]
    drawn = drawn.at[tuple(index_at)].set(low)
    longest = extent.index(max(extent))
    index_at[longest] = (index_at[longest] + 1) % extent[longest]
    return drawn.at[tuple(index_at)].set(top_value)


def block_levels(key, dims, cuts, least, largest):
    level = 1.0
    for axis_at, parts in cuts:
        steps = jax.random.uniform(jax.random.fold_in(jax.random.fold_in(key, 6), axis_at), (parts,), jnp.float32, least / len(cuts), largest / len(cuts))
        level = level * jnp.repeat(jnp.exp(steps), dims[axis_at] // parts).reshape((-1,) + (1,) * (len(dims) - 1 - axis_at))
    return level


def noise(own_key, extent, deviation, bound, cuts=(), kind=jnp.bfloat16):
    level = block_levels(own_key, extent, cuts, -0.22, 0.18) if cuts else 1.0
    drawn = jax.random.normal(own_key, extent, jnp.float32) * deviation * level
    return jnp.minimum(jnp.maximum(drawn, -bound), bound).astype(kind)


def setup_inputs(seed: int = 0) -> dict:
    arg_keys = jax.random.split(jax.random.key(seed), 10)
    return {
        "forcing": noise(arg_keys[0], (NY, NZ * COLS), 1.0, 6.0, ((0, 4), (1, 8)), jnp.float32),
        "start": noise(arg_keys[1], (NY, NZ * COLS), 0.3, 2.0, ((0, 4), (1, 8)), jnp.float32),
        "wall_even": noise(arg_keys[2], (HALF_NY, HALF_NY), HALF_NY ** -0.5, 0.3125, (), jnp.float32),
        "wall_odd": noise(arg_keys[3], (HALF_NY, HALF_NY), HALF_NY ** -0.5, 0.3125, (), jnp.float32),
        "diag_shift": jnp.clip(0.5 + 1.5 * jax.random.uniform(arg_keys[4], (NY, NZ), jnp.float32) ** block_levels(arg_keys[4], (NY, NZ), ((0, 4), (1, 8)), -0.2, 0.2), 0.5, 2.0),
        "band_coef": noise(arg_keys[5], (BANDS, NY, NZ), 0.3, 2.0, ((1, 4), (2, 8)), jnp.float32),
        "offsets": draw_offsets(jax.random.fold_in(arg_keys[9], 71), 0),
        "pattern": set_ends((jax.random.randint(arg_keys[7], (BANDS, NZ), 0, 4) < 3).astype(jnp.int32), jax.random.fold_in(arg_keys[7], 1), 0, 1),
        "block_inv": noise(arg_keys[8], (NY, WALL_ROWS), (16 * WALL_ROWS) ** -0.5, 0.109375, ((0, 4),), jnp.float32),
    }


def wall_term(field, wall_even, wall_odd):
    upper = field[:HALF_NY]
    lower = jnp.flip(field[HALF_NY:], 0)
    even_part = 0.5 * (upper + lower)
    odd_part = 0.5 * (upper - lower)
    first = jnp.dot(wall_even, even_part, precision=lax.Precision.HIGHEST, preferred_element_type=jnp.float32)
    second = jnp.dot(wall_odd, odd_part, precision=lax.Precision.HIGHEST, preferred_element_type=jnp.float32)
    return jnp.concatenate([first + second, jnp.flip(first - second, 0)], 0)


def span_term(field, diag_shift, band_coef, offsets, pattern):
    cube = field.reshape(NY, NZ, COLS)
    weights = band_coef * pattern.astype(jnp.float32)[:, None, :]
    result = diag_shift[:, :, None] * cube
    for band in range(BANDS):
        moved = jnp.roll(cube, -offsets[band], axis=1)
        result = result + weights[band][:, :, None] * moved
    return result.reshape(NY, NZ * COLS)


def reference(forcing, start, wall_even, wall_odd, diag_shift, band_coef, offsets, pattern, block_inv):
    solution = start
    residual = forcing
    blocks = block_inv.reshape(N_WALL, WALL_ROWS, WALL_ROWS).astype(jnp.float32)
    for sweep in range(SWEEPS):
        image = wall_term(solution, wall_even, wall_odd) + span_term(solution, diag_shift, band_coef, offsets, pattern)
        residual = forcing - image
        stacked = residual.reshape(N_WALL, WALL_ROWS, NZ * COLS)
        update = jnp.einsum("kij,kjw->kiw", blocks, stacked, precision=lax.Precision.HIGHEST)
        solution = solution + update.reshape(NY, NZ * COLS)
    return solution, residual
```

```python
import functools

import jax
import jax.numpy as jnp
from jax import lax
from jax.experimental import pallas as pl
from jax.experimental.pallas import tpu as pltpu
from jax.sharding import PartitionSpec as P

SWEEPS = 2
CHUNKS = 2
LANES = 128
SUB = 8
REACH = 2
SLOTS = 2 * (REACH + 1) + 1


def exchange(value, bit):
    count = lax.axis_size("wall")
    return lax.ppermute(value, "wall", [(i, i ^ bit) for i in range(count)])


def partner(value):
    count = lax.axis_size("span")
    return lax.ppermute(value, "span", [(i, i ^ 1) for i in range(count)])


def far(value, first):
    count = lax.axis_size("span")
    pairs = []
    for i in range(count):
        up = (i % 2 == 1) == first
        pairs.append((i, (i + (REACH if up else -REACH)) % count))
    return lax.ppermute(value, "span", pairs)


def params(**kw):
    return pltpu.CompilerParams(vmem_limit_bytes=kw.pop("vmem", 40 << 20), **kw)


def lane_iota():
    return lax.broadcasted_iota(jnp.int32, (SUB, LANES), 1)


def take(vec, index):
    return jnp.take_along_axis(vec, index, axis=1)


def split_kernel(chunks, width, x_ref, *out_refs):
    cw = width // chunks
    lane = lane_iota()
    per = LANES // width
    point = lane // cw
    rows = x_ref.shape[0]
    count = out_refs[0].shape[1] // LANES

    def step(i, _):
        here = pl.ds(pl.multiple_of(i * SUB, SUB), SUB)
        for j in range(count):
            source = [
                x_ref[here, (chunks * j + m) * LANES : (chunks * j + m + 1) * LANES]
                for m in range(chunks)
            ]
            for k in range(chunks):
                index = (point % per) * width + k * cw + lane % cw
                result = take(source[0], index)
                for m in range(1, chunks):
                    result = jnp.where(point // per == m, take(source[m], index), result)
                out_refs[k][here, j * LANES : (j + 1) * LANES] = result
        return 0

    lax.fori_loop(0, rows // SUB, step, 0)


def split(x, chunks, width):
    rows, breadth = x.shape
    out = jax.ShapeDtypeStruct((rows, breadth // chunks), x.dtype)
    return pl.pallas_call(
        functools.partial(split_kernel, chunks, width),
        out_shape=(out,) * chunks,
        compiler_params=params(),
        cost_estimate=pl.CostEstimate(flops=0, bytes_accessed=8 * rows * breadth, transcendentals=0),
        name="split",
    )(x)


def merged(parts, chunks, width, wide):
    cw = width // chunks
    lane = lane_iota()
    per = LANES // width
    per_chunk = LANES // cw
    j = wide // chunks
    base = (wide * per) % per_chunk
    index = (base + lane // width) * cw + lane % cw
    result = take(parts[0](j), index)
    for k in range(1, chunks):
        result = jnp.where((lane % width) // cw == k, take(parts[k](j), index), result)
    return result


def load_slots(ext_ref, pieces, slots, width):
    rows = ext_ref.shape[0]

    def clear(i, _):
        here = pl.ds(pl.multiple_of(i * SUB, SUB), SUB)
        ext_ref[here, :] = jnp.zeros((SUB, ext_ref.shape[1]), jnp.float32)
        for ref, slot in pieces:
            ext_ref[here, pl.ds(pl.multiple_of(slot * width, LANES), width)] = ref[here, :]
        return 0

    lax.fori_loop(0, rows // SUB, clear, 0)


def window(ext_ref, here, start, cw, count):
    per = LANES // cw
    base = pl.multiple_of(lax.div(start, per) * LANES, LANES)
    turn = lax.rem(start, per) * cw
    raw = [ext_ref[here, pl.ds(base + j * LANES, LANES)] for j in range(count + 1)]
    raw = [pltpu.roll(v, lax.rem(LANES - turn, LANES), 1) for v in raw]
    keep = lane_iota() < LANES - turn
    return [jnp.where(keep, raw[j], raw[j + 1]) for j in range(count)]


def weight(w_ref, here, row, points, cw, count):
    pack = LANES // points
    per = LANES // cw
    own = w_ref[row // pack, here, :]
    base = (row % pack) * points + lane_iota() // cw
    return [take(own, base + j * per) for j in range(count)]


def near_kernel(points, bands, cw, off_ref, sign_ref, x_ref, far_ref, w_ref, out_ref, ext_ref):
    count = out_ref.shape[1] // LANES
    sign = sign_ref[0]
    wide = x_ref.shape[1]
    center = REACH + 1
    load_slots(ext_ref, [(x_ref, center), (far_ref, center + 2 * sign)], SLOTS, wide)
    starts = [(center + sign) * points + off_ref[b] for b in range(bands)]

    def step(i, _):
        here = pl.ds(pl.multiple_of(i * SUB, SUB), SUB)
        total = None
        for b in range(bands):
            seen = window(ext_ref, here, starts[b], cw, count)
            scale = weight(w_ref, here, b, points, cw, count)
            terms = [s * v for s, v in zip(scale, seen)]
            total = terms if total is None else [t + u for t, u in zip(total, terms)]
        for j in range(count):
            out_ref[here, j * LANES : (j + 1) * LANES] = total[j]
        return 0

    lax.fori_loop(0, x_ref.shape[0] // SUB, step, 0)


SMEM = pl.BlockSpec(memory_space=pltpu.SMEM)
VMEM = pl.BlockSpec(memory_space=pltpu.VMEM)


def near(offsets, sign, x, first, w, points, cw):
    rows, wide = x.shape
    bands = offsets.shape[0]
    return pl.pallas_call(
        functools.partial(near_kernel, points, bands, cw),
        out_shape=jax.ShapeDtypeStruct(x.shape, x.dtype),
        in_specs=[SMEM, SMEM, VMEM, VMEM, VMEM],
        out_specs=VMEM,
        scratch_shapes=[pltpu.VMEM((rows, SLOTS * wide + LANES), jnp.float32)],
        compiler_params=params(),
        cost_estimate=pl.CostEstimate(
            flops=3000000000, bytes_accessed=4 * rows * wide * 4, transcendentals=0
        ),
        name="near",
    )(offsets, sign, x, first, w)


def halves(value):
    high = value.astype(jnp.bfloat16)
    low = (value - high.astype(jnp.float32)).astype(jnp.bfloat16)
    return high, low


def product(left_high, left_low, right):
    high, low = halves(right)
    dot = functools.partial(jnp.dot, preferred_element_type=jnp.float32)
    return dot(left_high, high) + (dot(left_high, low) + dot(left_low, high))


def middle_kernel(points, bands, cw, n_blocks, off_ref, sign_ref, f_ref, x_ref, far_ref, w_ref, mh_ref, ml_ref, *rest):
    others = rest[: n_blocks - 1]
    out_ref, ext_ref = rest[n_blocks - 1 :]
    count = out_ref.shape[1] // LANES
    sign = sign_ref[0]
    wide = x_ref.shape[1]
    center = REACH + 1
    tile = 2 * LANES
    blocks = (x_ref,) + tuple(others)

    def columns(n, _):
        at = pl.ds(pl.multiple_of(n * tile, tile), tile)
        total = f_ref[:, at]
        for k, ref in enumerate(blocks):
            total = total - product(mh_ref[k], ml_ref[k], ref[:, at])
        out_ref[:, at] = total
        return 0

    lax.fori_loop(0, wide // tile, columns, 0)
    load_slots(ext_ref, [(x_ref, center), (far_ref, center + 2 * sign)], SLOTS, wide)
    starts = [center * points + off_ref[b] for b in range(bands)]

    def step(i, _):
        here = pl.ds(pl.multiple_of(i * SUB, SUB), SUB)
        total = [out_ref[here, j * LANES : (j + 1) * LANES] for j in range(count)]
        scale = weight(w_ref, here, bands, points, cw, count)
        total = [t - s * x_ref[here, j * LANES : (j + 1) * LANES] for j, (t, s) in enumerate(zip(total, scale))]
        for b in range(bands):
            seen = window(ext_ref, here, starts[b], cw, count)
            scale = weight(w_ref, here, b, points, cw, count)
            total = [t - s * v for t, s, v in zip(total, scale, seen)]
        for j in range(count):
            out_ref[here, j * LANES : (j + 1) * LANES] = total[j]
        return 0

    lax.fori_loop(0, x_ref.shape[0] // SUB, step, 0)


def middle(offsets, sign, f, x, first, w, mh, ml, others, points, cw):
    rows, wide = x.shape
    bands = offsets.shape[0]
    n_blocks = len(others) + 1
    return pl.pallas_call(
        functools.partial(middle_kernel, points, bands, cw, n_blocks),
        out_shape=jax.ShapeDtypeStruct(x.shape, x.dtype),
        in_specs=[SMEM, SMEM] + [VMEM] * (6 + len(others)),
        out_specs=VMEM,
        scratch_shapes=[pltpu.VMEM((rows, SLOTS * wide + LANES), jnp.float32)],
        compiler_params=params(),
        cost_estimate=pl.CostEstimate(
            flops=6000000000, bytes_accessed=8 * rows * wide * 4, transcendentals=0
        ),
        name="middle",
    )(offsets, sign, f, x, first, w, mh, ml, *others)


def last_kernel(points, bands, cw, chunks, width, final, off_ref, sign_ref, g_ref, t_ref, x_ref, far_ref, w_ref, b_ref, *rest):
    earlier = rest[: 2 * (chunks - 1)] if final else ()
    rest = rest[len(earlier) :]
    sol_ref, res_ref = rest[0], rest[1]
    ext_ref, r_ref, x_new_ref = rest[2], rest[3], rest[4]
    rows, wide = x_ref.shape
    count = wide // LANES
    sign = sign_ref[0]
    load_slots(ext_ref, [(far_ref, 1)], 3, wide)

    def begin(i, _):
        here = pl.ds(pl.multiple_of(i * SUB, SUB), SUB)
        r_ref[here, :] = g_ref[here, :] - t_ref[here, :]
        return 0

    lax.fori_loop(0, rows // SUB, begin, 0)
    for b in range(bands):
        start = off_ref[b] + 2 * sign * points

        @pl.when(jnp.logical_and(start > -points, start < points))
        def _():
            def step(i, _):
                here = pl.ds(pl.multiple_of(i * SUB, SUB), SUB)
                seen = window(ext_ref, here, points + start, cw, count)
                scale = weight(w_ref, here, b, points, cw, count)
                for j in range(count):
                    at = slice(j * LANES, (j + 1) * LANES)
                    r_ref[here, at] = r_ref[here, at] - scale[j] * seen[j]
                return 0

            lax.fori_loop(0, rows // SUB, step, 0)

    bh, bl = halves(b_ref[...])
    tile = 2 * LANES
    target = x_new_ref if final else sol_ref

    def columns(n, _):
        at = pl.ds(pl.multiple_of(n * tile, tile), tile)
        target[:, at] = x_ref[:, at] + product(bh, bl, r_ref[:, at])
        return 0

    lax.fori_loop(0, wide // tile, columns, 0)
    if final:

        def join(i, _):
            here = pl.ds(pl.multiple_of(i * SUB, SUB), SUB)
            for which, (out_ref, own) in enumerate(((sol_ref, x_new_ref), (res_ref, r_ref))):
                refs = [earlier[2 * k + which] for k in range(chunks - 1)] + [own]
                parts = [lambda j, ref=ref: ref[here, j * LANES : (j + 1) * LANES] for ref in refs]
                for wide_at in range(count * chunks):
                    out_ref[here, wide_at * LANES : (wide_at + 1) * LANES] = merged(parts, chunks, width, wide_at)
            return 0

        lax.fori_loop(0, rows // SUB, join, 0)
    else:

        @pl.when(sign == sign)
        def _():
            res_ref[...] = r_ref[...]


def last(offsets, sign, g, t, x, second, w, b, earlier, points, cw, chunks, width, final):
    rows, wide = x.shape
    bands = offsets.shape[0]
    out_wide = wide * chunks if final else wide
    out = jax.ShapeDtypeStruct((rows, out_wide), x.dtype)
    return pl.pallas_call(
        functools.partial(last_kernel, points, bands, cw, chunks, width, final),
        out_shape=(out, out),
        in_specs=[SMEM, SMEM] + [VMEM] * (6 + len(earlier)),
        out_specs=(VMEM, VMEM),
        scratch_shapes=[
            pltpu.VMEM((rows, 3 * wide + LANES), jnp.float32),
            pltpu.VMEM((rows, wide), jnp.float32),
            pltpu.VMEM((rows, wide) if final else (SUB, LANES), jnp.float32),
        ],
        compiler_params=params(),
        cost_estimate=pl.CostEstimate(
            flops=3000000000, bytes_accessed=8 * rows * wide * 4, transcendentals=0
        ),
        name="last",
    )(offsets, sign, g, t, x, second, w, b, *earlier)


def wall_rows(wall_even, wall_odd, rows):
    count = lax.axis_size("wall")
    total = count * rows
    half = total // 2
    index = lax.axis_index("wall")
    upper = index < count // 2
    at = jnp.where(upper, index, count - 1 - index) * rows
    even = lax.dynamic_slice_in_dim(wall_even, at, rows, 0)
    odd = lax.dynamic_slice_in_dim(wall_odd, at, rows, 0)
    same = 0.5 * (even + odd)
    cross = 0.5 * (even - odd)
    full = jnp.concatenate([same, jnp.flip(cross, 1)], 1)
    full = jnp.where(upper, full, jnp.flip(full, (0, 1)))
    blocks = jnp.stack([full[:, k * rows : (k + 1) * rows] for k in range(count)])
    ordered = jnp.stack([lax.dynamic_index_in_dim(blocks, index ^ k, 0, False) for k in range(count)])
    high = lax.reduce_precision(ordered, 8, 7)
    return high.astype(jnp.bfloat16), (ordered - high).astype(jnp.bfloat16)


def after(value, *others):
    return lax.optimization_barrier((value, *others))[0]


def shards(forcing, start, wall_even, wall_odd, diag_shift, band_coef, offsets, pattern, block_inv):
    rows, breadth = start.shape
    points = diag_shift.shape[1]
    bands = band_coef.shape[0]
    width = breadth // points
    chunks = CHUNKS
    cw = width // chunks
    n_wall = lax.axis_size("wall")
    sign = jnp.where(lax.axis_index("span") % 2 == 0, 1, -1).astype(jnp.int32)[None]

    state = list(split(start, chunks, width))
    pack = LANES // points
    scaled = band_coef * pattern.astype(jnp.float32)[:, None, :]
    stacked = jnp.concatenate([scaled, diag_shift[None], jnp.zeros((-(bands + 1) % pack, rows, points), jnp.float32)], 0)
    own_w = jnp.concatenate([stacked[k::pack] for k in range(pack)], 2)
    their_w = partner(own_w[: bands // pack])
    mh, ml = wall_rows(wall_even, wall_odd, rows)
    f = split(forcing, chunks, width)
    residual = [None] * chunks
    for sweep in range(SWEEPS):
        final_sweep = sweep == SWEEPS - 1
        firsts = [far(state[k], True) for k in range(chunks)]
        walls = []
        for k in range(chunks):
            got = [state[k]]
            bit = n_wall // 2
            while bit:
                got = got + [exchange(v, bit) for v in got]
                bit //= 2
            walls.append(got)
        order = [0]
        bit = n_wall // 2
        while bit:
            order = order + [o ^ bit for o in order]
            bit //= 2
        theirs = []
        seconds = []
        for k in range(chunks):
            partial = near(offsets, sign, state[k], firsts[k], their_w, points, cw)
            theirs.append(partner(partial))
            seconds.append(far(after(state[k], firsts[k]), False))
        new = []
        for k in range(chunks):
            others = [walls[k][order.index(o)] for o in range(1, n_wall)]
            g = middle(offsets, sign, f[k], state[k], firsts[k], own_w, mh, ml, others, points, cw)
            final = final_sweep and k == chunks - 1
            earlier = [a for pair in new for a in pair] if final else []
            new.append(
                last(offsets, sign, g, theirs[k], state[k], seconds[k], own_w, block_inv, earlier, points, cw, chunks, width, final)
            )
        state = [pair[0] for pair in new]
        residual = [pair[1] for pair in new]
    return state[-1], residual[-1]


def solution(mesh):
    in_specs = (
        P("wall", "span"),
        P("wall", "span"),
        P(),
        P(),
        P("wall", "span"),
        P(None, "wall", "span"),
        P(),
        P(None, "span"),
        P("wall", None),
    )
    out_specs = (P("wall", "span"), P("wall", "span"))
    return jax.shard_map(shards, mesh=mesh, in_specs=in_specs, out_specs=out_specs, check_vma=False)
```

```python
import functools

import jax
import jax.numpy as jnp
from jax import lax
from jax.experimental import pallas as pl
from jax.experimental.pallas import tpu as pltpu
from jax.sharding import PartitionSpec as P

SWEEPS = 2
CHUNKS = 2
LANES = 128
HALF = LANES // 2
REACH = 2


def exchange(value, bit):
    count = lax.axis_size("wall")
    return lax.ppermute(value, "wall", [(i, i ^ bit) for i in range(count)])


def partner(value):
    count = lax.axis_size("span")
    return lax.ppermute(value, "span", [(i, i ^ 1) for i in range(count)])


def far(value, first):
    count = lax.axis_size("span")
    pairs = []
    for i in range(count):
        up = (i % 2 == 1) == first
        pairs.append((i, (i + (REACH if up else -REACH)) % count))
    return lax.ppermute(value, "span", pairs)


def params():
    return pltpu.CompilerParams(vmem_limit_bytes=40 << 20)


SMEM = pl.BlockSpec(memory_space=pltpu.SMEM)
VMEM = pl.BlockSpec(memory_space=pltpu.VMEM)


def split_kernel(width, x_ref, *out_refs):
    chunks = len(out_refs)
    cw = width // chunks
    half = cw // 2
    per = LANES // width

    def step(g, _):
        lanes = pl.ds(pl.multiple_of(g * LANES, LANES), LANES)
        top = x_ref[:LANES, lanes].T.reshape(per, width, LANES)
        low = x_ref[LANES:, lanes]
        pair = jnp.concatenate([low, pltpu.roll(low, LANES - half, 1)], 0)
        pair = pair.T.reshape(per, width, LANES)
        here = pl.ds(g * per, per)
        for k, out_ref in enumerate(out_refs):
            out_ref[here, :cw, :] = top[:, k * cw : (k + 1) * cw, :]
            out_ref[here, cw:, :] = pair[:, k * cw : k * cw + half, :]
        return 0

    lax.fori_loop(0, x_ref.shape[1] // LANES, step, 0)


def split(x, chunks, points):
    rows, breadth = x.shape
    width = breadth // points
    cw = width // chunks
    out = jax.ShapeDtypeStruct((points, cw + cw // 2, LANES), x.dtype)
    return pl.pallas_call(
        functools.partial(split_kernel, width),
        out_shape=(out,) * chunks,
        in_specs=[VMEM],
        out_specs=(VMEM,) * chunks,
        compiler_params=params(),
        cost_estimate=pl.CostEstimate(flops=0, bytes_accessed=8 * rows * breadth, transcendentals=0),
        name="split",
    )(x)


def join(width, sol_parts, res_parts, sol_ref, res_ref):
    chunks = len(sol_parts)
    cw = width // chunks
    half = cw // 2
    per = LANES // width
    lower = lax.broadcasted_iota(jnp.int32, (half, LANES), 1) < HALF

    def step(g, _):
        lanes = pl.ds(pl.multiple_of(g * LANES, LANES), LANES)
        for out_ref, parts in ((sol_ref, sol_parts), (res_ref, res_parts)):
            rows = [part[g * per + z, :cw, :] for z in range(per) for part in parts]
            out_ref[:LANES, lanes] = jnp.concatenate(rows, 0).T
        rows = []
        for z in range(per):
            for sol, res in zip(sol_parts, res_parts):
                a = sol[g * per + z, cw:, :]
                b = res[g * per + z, cw:, :]
                rows.append(jnp.where(lower, a, pltpu.roll(b, HALF, 1)))
                rows.append(jnp.where(lower, pltpu.roll(a, HALF, 1), b))
        both = jnp.concatenate(rows, 0).T
        sol_ref[LANES:, lanes] = both[:HALF]
        res_ref[LANES:, lanes] = both[HALF:]
        return 0

    lax.fori_loop(0, sol_ref.shape[1] // LANES, step, 0)


UNROLL = 4


def fill(ext_ref, pieces, points):
    def step(i, _):
        for slot in range(ext_ref.shape[0] // points):
            here = pl.ds(slot * points + i * UNROLL, UNROLL)
            ext_ref[here] = jnp.zeros((UNROLL, *ext_ref.shape[1:]), jnp.float32)
        return 0

    lax.fori_loop(0, points // UNROLL, step, 0)

    def copy(i, _):
        for ref, slot in pieces:
            ext_ref[pl.ds(slot * points + i * UNROLL, UNROLL)] = ref[pl.ds(i * UNROLL, UNROLL)]
        return 0

    lax.fori_loop(0, points // UNROLL, copy, 0)


def scaled(w_ref, row, value, cw):
    top = w_ref[0, pl.ds(row, 1), :] * value[:cw]
    low = w_ref[1, pl.ds(row, 1), :] * value[cw:]
    return top, low


def near_kernel(bands, off_ref, sign_ref, x_ref, far_ref, w_ref, theirs_ref, partial_ref, sum_ref, ext_ref):
    points, rows, _ = x_ref.shape
    cw = rows * 2 // 3
    sign = sign_ref[0]
    own = jnp.where(sign > 0, REACH, REACH + 1)
    fill(ext_ref, [(x_ref, own), (far_ref, own + 2 * sign)], points)

    for out_ref, weights, shift in ((partial_ref, theirs_ref, sign), (sum_ref, w_ref, 0)):
        starts = [(own + shift) * points + off_ref[b] for b in range(bands)]

        def step(i, _):
            for u in range(UNROLL):
                p = i * UNROLL + u
                if out_ref is sum_ref:
                    top, low = scaled(weights, bands * points + p, x_ref[p], cw)
                else:
                    top, low = None, None
                for b in range(bands):
                    t, l = scaled(weights, b * points + p, ext_ref[starts[b] + p], cw)
                    top, low = (t, l) if top is None else (top + t, low + l)
                out_ref[p, :cw, :] = top
                out_ref[p, cw:, :] = low
            return 0

        lax.fori_loop(0, points // UNROLL, step, 0)


def near(offsets, sign, x, first, w, theirs):
    bands = offsets.shape[0]
    points, rows, _ = x.shape
    out = jax.ShapeDtypeStruct(x.shape, x.dtype)
    return pl.pallas_call(
        functools.partial(near_kernel, bands),
        out_shape=(out, out),
        in_specs=[SMEM, SMEM, VMEM, VMEM, VMEM, VMEM],
        out_specs=(VMEM, VMEM),
        scratch_shapes=[pltpu.VMEM(((2 * REACH + 2) * points, rows, LANES), jnp.float32)],
        compiler_params=params(),
        cost_estimate=pl.CostEstimate(flops=1000000000, bytes_accessed=6 * x.size * 4, transcendentals=0),
        name="near",
    )(offsets, sign, x, first, w, theirs)


def halves(value):
    high = value.astype(jnp.bfloat16)
    low = (value - high.astype(jnp.float32)).astype(jnp.bfloat16)
    return high, low


def product(high, low, w_high, w_low):
    dot = functools.partial(jnp.dot, preferred_element_type=jnp.float32)
    return dot(high, w_high) + (dot(low, w_high) + dot(high, w_low))


def stage(high_ref, low_ref, at, ref, cw):
    points = ref.shape[0]
    half = cw // 2
    count = points * half
    low = ref[:, cw:, :].reshape(count, LANES)
    turned = pltpu.roll(low, HALF, 1)
    for part, top, rest in ((0, ref[:, :half, :], low), (1, ref[:, half:cw, :], turned)):
        rows = slice(part * count, (part + 1) * count)
        for n, value in enumerate((top.reshape(count, LANES), rest)):
            columns = slice(at + n * LANES, at + (n + 1) * LANES)
            high, small = halves(value)
            high_ref[rows, columns] = high
            low_ref[rows, columns] = small


def unstage(value, points, cw):
    half = cw // 2
    count = points * half
    first, second = value[:count], value[count:]
    top = [v[:, :LANES].reshape(points, half, LANES) for v in (first, second)]
    low = first[:, LANES:] + pltpu.roll(second[:, LANES:], HALF, 1)
    return top, low.reshape(points, half, LANES)


def wall_kernel(n_blocks, f_ref, mh_ref, ml_ref, *rest):
    blocks = rest[:n_blocks]
    out_ref, high_ref, low_ref = rest[n_blocks:]
    points, rows, _ = f_ref.shape
    cw = rows * 2 // 3
    half = cw // 2
    for k, ref in enumerate(blocks):
        stage(high_ref, low_ref, 2 * LANES * k, ref, cw)
    result = product(high_ref[...], low_ref[...], mh_ref[...], ml_ref[...])
    top, low = unstage(result, points, cw)
    out_ref[:, :half, :] = f_ref[:, :half, :] - top[0]
    out_ref[:, half:cw, :] = f_ref[:, half:cw, :] - top[1]
    out_ref[:, cw:, :] = f_ref[:, cw:, :] - low


def wall(f, mh, ml, blocks):
    points, rows, _ = f.shape
    n_blocks = len(blocks)
    m_rows = points * rows * 2 // 3
    return pl.pallas_call(
        functools.partial(wall_kernel, n_blocks),
        out_shape=jax.ShapeDtypeStruct(f.shape, f.dtype),
        in_specs=[VMEM] * (3 + n_blocks),
        out_specs=VMEM,
        scratch_shapes=[pltpu.VMEM((m_rows, 2 * LANES * n_blocks), jnp.bfloat16)] * 2,
        compiler_params=params(),
        cost_estimate=pl.CostEstimate(flops=3000000000, bytes_accessed=8 * f.size * 4, transcendentals=0),
        name="wall",
    )(f, mh, ml, *blocks)


def last_kernel(bands, width, n_earlier, off_ref, sign_ref, g_ref, s_ref, t_ref, x_ref, far_ref, w_ref, bh_ref, bl_ref, *rest):
    earlier = rest[: 2 * n_earlier]
    rest = rest[2 * n_earlier :]
    if width:
        sol_ref, res_ref, ext_ref, high_ref, low_ref, x_new_ref, r_ref = rest
    else:
        x_new_ref, r_ref, ext_ref, high_ref, low_ref = rest
    points, rows, _ = x_ref.shape
    cw = rows * 2 // 3
    half = cw // 2
    sign = sign_ref[0]
    fill(ext_ref, [(far_ref, 1)], points)

    def begin(i, _):
        here = pl.ds(i * UNROLL, UNROLL)
        r_ref[here] = g_ref[here] - s_ref[here] - t_ref[here]
        return 0

    lax.fori_loop(0, points // UNROLL, begin, 0)
    for b in range(bands):
        start = off_ref[b] + 2 * sign * points

        @pl.when(jnp.logical_and(start > -points, start < points))
        def _():
            def step(i, _):
                for u in range(UNROLL):
                    p = i * UNROLL + u
                    top, low = scaled(w_ref, b * points + p, ext_ref[points + start + p], cw)
                    r_ref[p, :cw, :] = r_ref[p, :cw, :] - top
                    r_ref[p, cw:, :] = r_ref[p, cw:, :] - low
                return 0

            lax.fori_loop(0, points // UNROLL, step, 0)

    stage(high_ref, low_ref, 0, r_ref, cw)
    result = product(high_ref[...], low_ref[...], bh_ref[...], bl_ref[...])
    top, low = unstage(result, points, cw)
    x_new_ref[:, :half, :] = x_ref[:, :half, :] + top[0]
    x_new_ref[:, half:cw, :] = x_ref[:, half:cw, :] + top[1]
    x_new_ref[:, cw:, :] = x_ref[:, cw:, :] + low
    if width:
        join(width, [*earlier[::2], x_new_ref], [*earlier[1::2], r_ref], sol_ref, res_ref)


def last(offsets, sign, g, s, t, x, second, w, bh, bl, earlier, width):
    bands = offsets.shape[0]
    points, rows, _ = x.shape
    chunk = pltpu.VMEM(x.shape, jnp.float32)
    if width:
        out = jax.ShapeDtypeStruct((LANES + HALF, points * width), x.dtype)
    else:
        out = jax.ShapeDtypeStruct(x.shape, x.dtype)
    m_rows = points * rows * 2 // 3
    return pl.pallas_call(
        functools.partial(last_kernel, bands, width, len(earlier) // 2),
        out_shape=(out, out),
        in_specs=[SMEM, SMEM] + [VMEM] * (8 + len(earlier)),
        out_specs=(VMEM, VMEM),
        scratch_shapes=[
            pltpu.VMEM((3 * points, rows, LANES), jnp.float32),
            pltpu.VMEM((m_rows, 2 * LANES), jnp.bfloat16),
            pltpu.VMEM((m_rows, 2 * LANES), jnp.bfloat16),
        ]
        + ([chunk, chunk] if width else []),
        compiler_params=params(),
        cost_estimate=pl.CostEstimate(flops=1000000000, bytes_accessed=8 * x.size * 4, transcendentals=0),
        name="last",
    )(offsets, sign, g, s, t, x, second, w, bh, bl, *earlier)


def two_parts(value):
    high = lax.reduce_precision(value, 8, 7)
    return high.astype(jnp.bfloat16), (value - high).astype(jnp.bfloat16)


def right_side(matrix):
    rows = matrix.shape[0]
    return jnp.pad(matrix.T, ((0, 2 * LANES - rows), (0, 2 * LANES - rows)))


def wall_rows(wall_even, wall_odd, rows):
    count = lax.axis_size("wall")
    index = lax.axis_index("wall")
    upper = index < count // 2
    at = jnp.where(upper, index, count - 1 - index) * rows
    even = lax.dynamic_slice_in_dim(wall_even, at, rows, 0)
    odd = lax.dynamic_slice_in_dim(wall_odd, at, rows, 0)
    same = 0.5 * (even + odd)
    cross = 0.5 * (even - odd)
    full = jnp.concatenate([same, jnp.flip(cross, 1)], 1)
    full = jnp.where(upper, full, jnp.flip(full, (0, 1)))
    blocks = jnp.stack([right_side(full[:, k * rows : (k + 1) * rows]) for k in range(count)])
    ordered = jnp.concatenate([lax.dynamic_index_in_dim(blocks, index ^ k, 0, False) for k in range(count)], 0)
    return two_parts(ordered)


def after(value, *others):
    return lax.optimization_barrier((value, *others))[0]


def shards(forcing, start, wall_even, wall_odd, diag_shift, band_coef, offsets, pattern, block_inv):
    rows, breadth = start.shape
    points = diag_shift.shape[1]
    bands = band_coef.shape[0]
    width = breadth // points
    chunks = CHUNKS
    n_wall = lax.axis_size("wall")
    sign = jnp.where(lax.axis_index("span") % 2 == 0, 1, -1).astype(jnp.int32)[None]

    state = list(split(start, chunks, points))
    weights = jnp.swapaxes(band_coef, 1, 2) * pattern.astype(jnp.float32)[:, :, None]
    weights = jnp.concatenate([weights, diag_shift.T[None]], 0).reshape((bands + 1) * points, rows)
    low = weights[:, LANES:]
    own_w = jnp.stack([weights[:, :LANES], jnp.concatenate([low, low], 1)])
    their_w = partner(own_w[:, : bands * points])
    mh, ml = wall_rows(wall_even, wall_odd, rows)
    bh, bl = two_parts(right_side(block_inv))
    f = split(forcing, chunks, points)
    residual = [None] * chunks
    order = [0]
    bit = n_wall // 2
    while bit:
        order = order + [o ^ bit for o in order]
        bit //= 2
    for sweep in range(SWEEPS):
        final_sweep = sweep == SWEEPS - 1
        firsts = [far(state[k], True) for k in range(chunks)]
        walls = []
        for k in range(chunks):
            got = [state[k]]
            bit = n_wall // 2
            while bit:
                got = got + [exchange(v, bit) for v in got]
                bit //= 2
            walls.append([got[order.index(o)] for o in range(n_wall)])
        theirs = []
        sums = []
        seconds = []
        for k in range(chunks):
            partial, own_sum = near(offsets, sign, state[k], firsts[k], own_w, their_w)
            sums.append(own_sum)
            theirs.append(partner(partial))
            seconds.append(far(after(state[k], firsts[k]), False))
        new = []
        for k in range(chunks):
            g = wall(f[k], mh, ml, walls[k])
            final = final_sweep and k == chunks - 1
            earlier = [a for pair in new for a in pair] if final else []
            new.append(
                last(offsets, sign, g, sums[k], theirs[k], state[k], seconds[k], own_w, bh, bl, earlier, width if final else 0)
            )
        state = [pair[0] for pair in new]
        residual = [pair[1] for pair in new]
    return state[-1], residual[-1]


def solution(mesh):
    in_specs = (
        P("wall", "span"),
        P("wall", "span"),
        P(),
        P(),
        P("wall", "span"),
        P(None, "wall", "span"),
        P(),
        P(None, "span"),
        P("wall", None),
    )
    out_specs = (P("wall", "span"), P("wall", "span"))
    return jax.shard_map(shards, mesh=mesh, in_specs=in_specs, out_specs=out_specs, check_vma=False)
```

```python
import functools

import jax
import jax.numpy as jnp
from jax import lax
from jax.experimental import pallas as pl
from jax.experimental.pallas import tpu as pltpu
from jax.sharding import PartitionSpec as P


SWEEPS = 2
CHUNKS = 2
LANES = 128
HALF = LANES // 2
REACH = 2


def exchange(value, bit):
    count = lax.axis_size("wall")
    return lax.ppermute(value, "wall", [(i, i ^ bit) for i in range(count)])


def partner(value):
    count = lax.axis_size("span")
    return lax.ppermute(value, "span", [(i, i ^ 1) for i in range(count)])


def far(value, first):
    count = lax.axis_size("span")
    pairs = []
    for i in range(count):
        up = (i % 2 == 1) == first
        pairs.append((i, (i + (REACH if up else -REACH)) % count))
    return lax.ppermute(value, "span", pairs)


def params():
    return pltpu.CompilerParams(vmem_limit_bytes=40 << 20)


SMEM = pl.BlockSpec(memory_space=pltpu.SMEM)
VMEM = pl.BlockSpec(memory_space=pltpu.VMEM)


def split_kernel(width, x_ref, *out_refs):
    chunks = len(out_refs)
    cw = width // chunks
    half = cw // 2
    per = LANES // width

    def step(g, _):
        lanes = pl.ds(pl.multiple_of(g * LANES, LANES), LANES)
        top = x_ref[:LANES, lanes].T.reshape(per, width, LANES)
        low = x_ref[LANES:, lanes]
        pair = jnp.concatenate([low, pltpu.roll(low, LANES - half, 1)], 0)
        pair = pair.T.reshape(per, width, LANES)
        here = pl.ds(g * per, per)
        for k, out_ref in enumerate(out_refs):
            out_ref[here, :cw, :] = top[:, k * cw : (k + 1) * cw, :]
            out_ref[here, cw:, :] = pair[:, k * cw : k * cw + half, :]
        return 0

    lax.fori_loop(0, x_ref.shape[1] // LANES, step, 0)


def split(x, chunks, points):
    rows, breadth = x.shape
    width = breadth // points
    cw = width // chunks
    out = jax.ShapeDtypeStruct((points, cw + cw // 2, LANES), x.dtype)
    return pl.pallas_call(
        functools.partial(split_kernel, width),
        out_shape=(out,) * chunks,
        in_specs=[VMEM],
        out_specs=(VMEM,) * chunks,
        compiler_params=params(),
        cost_estimate=pl.CostEstimate(flops=0, bytes_accessed=8 * rows * breadth, transcendentals=0),
        name="split",
    )(x)


def join(width, sol_parts, res_parts, sol_ref, res_ref):
    chunks = len(sol_parts)
    cw = width // chunks
    half = cw // 2
    per = LANES // width
    lower = lax.broadcasted_iota(jnp.int32, (half, LANES), 1) < HALF

    def step(g, _):
        lanes = pl.ds(pl.multiple_of(g * LANES, LANES), LANES)
        for out_ref, parts in ((sol_ref, sol_parts), (res_ref, res_parts)):
            rows = [part[g * per + z, :cw, :] for z in range(per) for part in parts]
            out_ref[:LANES, lanes] = jnp.concatenate(rows, 0).T
        rows = []
        for z in range(per):
            for sol, res in zip(sol_parts, res_parts):
                a = sol[g * per + z, cw:, :]
                b = res[g * per + z, cw:, :]
                rows.append(jnp.where(lower, a, pltpu.roll(b, HALF, 1)))
                rows.append(jnp.where(lower, pltpu.roll(a, HALF, 1), b))
        both = jnp.concatenate(rows, 0).T
        sol_ref[LANES:, lanes] = both[:HALF]
        res_ref[LANES:, lanes] = both[HALF:]
        return 0

    lax.fori_loop(0, sol_ref.shape[1] // LANES, step, 0)


UNROLL = 4


def fill(ext_ref, pieces, points):
    def step(i, _):
        for slot in range(ext_ref.shape[0] // points):
            here = pl.ds(slot * points + i * UNROLL, UNROLL)
            ext_ref[here] = jnp.zeros((UNROLL, *ext_ref.shape[1:]), jnp.float32)
        return 0

    lax.fori_loop(0, points // UNROLL, step, 0)

    def copy(i, _):
        for ref, slot in pieces:
            ext_ref[pl.ds(slot * points + i * UNROLL, UNROLL)] = ref[pl.ds(i * UNROLL, UNROLL)]
        return 0

    lax.fori_loop(0, points // UNROLL, copy, 0)


def scaled(w_ref, row, value, cw):
    top = w_ref[0, pl.ds(row, 1), :] * value[:cw]
    low = w_ref[1, pl.ds(row, 1), :] * value[cw:]
    return top, low


def near_kernel(bands, off_ref, sign_ref, x_ref, far_ref, w_ref, theirs_ref, partial_ref, sum_ref, ext_ref):
    points, rows, _ = x_ref.shape
    cw = rows * 2 // 3
    sign = sign_ref[0]
    own = jnp.where(sign > 0, REACH, REACH + 1)
    fill(ext_ref, [(x_ref, own), (far_ref, own + 2 * sign)], points)

    for out_ref, weights, shift in ((partial_ref, theirs_ref, sign), (sum_ref, w_ref, 0)):
        starts = [(own + shift) * points + off_ref[b] for b in range(bands)]

        def step(i, _):
            for u in range(UNROLL):
                p = i * UNROLL + u
                if out_ref is sum_ref:
                    top, low = scaled(weights, bands * points + p, x_ref[p], cw)
                else:
                    top, low = None, None
                for b in range(bands):
                    t, l = scaled(weights, b * points + p, ext_ref[starts[b] + p], cw)
                    top, low = (t, l) if top is None else (top + t, low + l)
                out_ref[p, :cw, :] = top
                out_ref[p, cw:, :] = low
            return 0

        lax.fori_loop(0, points // UNROLL, step, 0)


def near(offsets, sign, x, first, w, theirs):
    bands = offsets.shape[0]
    points, rows, _ = x.shape
    out = jax.ShapeDtypeStruct(x.shape, x.dtype)
    return pl.pallas_call(
        functools.partial(near_kernel, bands),
        out_shape=(out, out),
        in_specs=[SMEM, SMEM, VMEM, VMEM, VMEM, VMEM],
        out_specs=(VMEM, VMEM),
        scratch_shapes=[pltpu.VMEM(((2 * REACH + 2) * points, rows, LANES), jnp.float32)],
        compiler_params=params(),
        cost_estimate=pl.CostEstimate(flops=1000000000, bytes_accessed=6 * x.size * 4, transcendentals=0),
        name="near",
    )(offsets, sign, x, first, w, theirs)


def halves(value):
    high = value.astype(jnp.bfloat16)
    low = (value - high.astype(jnp.float32)).astype(jnp.bfloat16)
    return high, low


def product(high, low, w_high, w_low):
    dot = functools.partial(jnp.dot, preferred_element_type=jnp.float32)
    return dot(high, w_high) + (dot(low, w_high) + dot(high, w_low))


def stage(high_ref, low_ref, at, ref, cw):
    points = ref.shape[0]
    half = cw // 2
    count = points * half
    low = ref[:, cw:, :].reshape(count, LANES)
    turned = pltpu.roll(low, HALF, 1)
    for part, top, rest in ((0, ref[:, :half, :], low), (1, ref[:, half:cw, :], turned)):
        rows = slice(part * count, (part + 1) * count)
        for n, value in enumerate((top.reshape(count, LANES), rest)):
            columns = slice(at + n * LANES, at + (n + 1) * LANES)
            high, small = halves(value)
            high_ref[rows, columns] = high
            low_ref[rows, columns] = small


def unstage(value, points, cw):
    half = cw // 2
    count = points * half
    first, second = value[:count], value[count:]
    top = [v[:, :LANES].reshape(points, half, LANES) for v in (first, second)]
    low = first[:, LANES:] + pltpu.roll(second[:, LANES:], HALF, 1)
    return top, low.reshape(points, half, LANES)


def wall_kernel(n_blocks, f_ref, mh_ref, ml_ref, *rest):
    blocks = rest[:n_blocks]
    out_ref, high_ref, low_ref = rest[n_blocks:]
    points, rows, _ = f_ref.shape
    cw = rows * 2 // 3
    half = cw // 2
    for k, ref in enumerate(blocks):
        stage(high_ref, low_ref, 2 * LANES * k, ref, cw)
    result = product(high_ref[...], low_ref[...], mh_ref[...], ml_ref[...])
    top, low = unstage(result, points, cw)
    out_ref[:, :half, :] = f_ref[:, :half, :] - top[0]
    out_ref[:, half:cw, :] = f_ref[:, half:cw, :] - top[1]
    out_ref[:, cw:, :] = f_ref[:, cw:, :] - low


def wall(f, mh, ml, blocks):
    points, rows, _ = f.shape
    n_blocks = len(blocks)
    m_rows = points * rows * 2 // 3
    return pl.pallas_call(
        functools.partial(wall_kernel, n_blocks),
        out_shape=jax.ShapeDtypeStruct(f.shape, f.dtype),
        in_specs=[VMEM] * (3 + n_blocks),
        out_specs=VMEM,
        scratch_shapes=[pltpu.VMEM((m_rows, 2 * LANES * n_blocks), jnp.bfloat16)] * 2,
        compiler_params=params(),
        cost_estimate=pl.CostEstimate(flops=3000000000, bytes_accessed=8 * f.size * 4, transcendentals=0),
        name="wall",
    )(f, mh, ml, *blocks)


def last_kernel(bands, width, n_earlier, off_ref, sign_ref, g_ref, s_ref, t_ref, x_ref, far_ref, w_ref, bh_ref, bl_ref, *rest):
    earlier = rest[: 2 * n_earlier]
    rest = rest[2 * n_earlier :]
    if width:
        sol_ref, res_ref, ext_ref, high_ref, low_ref, x_new_ref, r_ref = rest
    else:
        x_new_ref, r_ref, ext_ref, high_ref, low_ref = rest
    points, rows, _ = x_ref.shape
    cw = rows * 2 // 3
    half = cw // 2
    sign = sign_ref[0]
    fill(ext_ref, [(far_ref, 1)], points)

    def begin(i, _):
        here = pl.ds(i * UNROLL, UNROLL)
        r_ref[here] = g_ref[here] - s_ref[here] - t_ref[here]
        return 0

    lax.fori_loop(0, points // UNROLL, begin, 0)
    for b in range(bands):
        start = off_ref[b] + 2 * sign * points

        @pl.when(jnp.logical_and(start > -points, start < points))
        def _():
            def step(i, _):
                for u in range(UNROLL):
                    p = i * UNROLL + u
                    top, low = scaled(w_ref, b * points + p, ext_ref[points + start + p], cw)
                    r_ref[p, :cw, :] = r_ref[p, :cw, :] - top
                    r_ref[p, cw:, :] = r_ref[p, cw:, :] - low
                return 0

            lax.fori_loop(0, points // UNROLL, step, 0)

    stage(high_ref, low_ref, 0, r_ref, cw)
    result = product(high_ref[...], low_ref[...], bh_ref[...], bl_ref[...])
    top, low = unstage(result, points, cw)
    x_new_ref[:, :half, :] = x_ref[:, :half, :] + top[0]
    x_new_ref[:, half:cw, :] = x_ref[:, half:cw, :] + top[1]
    x_new_ref[:, cw:, :] = x_ref[:, cw:, :] + low
    if width:
        join(width, [*earlier[::2], x_new_ref], [*earlier[1::2], r_ref], sol_ref, res_ref)


def last(offsets, sign, g, s, t, x, second, w, bh, bl, earlier, width):
    bands = offsets.shape[0]
    points, rows, _ = x.shape
    chunk = pltpu.VMEM(x.shape, jnp.float32)
    if width:
        out = jax.ShapeDtypeStruct((LANES + HALF, points * width), x.dtype)
    else:
        out = jax.ShapeDtypeStruct(x.shape, x.dtype)
    m_rows = points * rows * 2 // 3
    return pl.pallas_call(
        functools.partial(last_kernel, bands, width, len(earlier) // 2),
        out_shape=(out, out),
        in_specs=[SMEM, SMEM] + [VMEM] * (8 + len(earlier)),
        out_specs=(VMEM, VMEM),
        scratch_shapes=[
            pltpu.VMEM((3 * points, rows, LANES), jnp.float32),
            pltpu.VMEM((m_rows, 2 * LANES), jnp.bfloat16),
            pltpu.VMEM((m_rows, 2 * LANES), jnp.bfloat16),
        ]
        + ([chunk, chunk] if width else []),
        compiler_params=params(),
        cost_estimate=pl.CostEstimate(flops=1000000000, bytes_accessed=8 * x.size * 4, transcendentals=0),
        name="last",
    )(offsets, sign, g, s, t, x, second, w, bh, bl, *earlier)


def two_parts(value):
    high = lax.reduce_precision(value, 8, 7)
    return high.astype(jnp.bfloat16), (value - high).astype(jnp.bfloat16)


def right_side(matrix):
    rows = matrix.shape[0]
    return jnp.pad(matrix.T, ((0, 2 * LANES - rows), (0, 2 * LANES - rows)))


def wall_rows(wall_even, wall_odd, rows):
    count = lax.axis_size("wall")
    index = lax.axis_index("wall")
    upper = index < count // 2
    at = jnp.where(upper, index, count - 1 - index) * rows
    even = lax.dynamic_slice_in_dim(wall_even, at, rows, 0)
    odd = lax.dynamic_slice_in_dim(wall_odd, at, rows, 0)
    same = 0.5 * (even + odd)
    cross = 0.5 * (even - odd)
    full = jnp.concatenate([same, jnp.flip(cross, 1)], 1)
    full = jnp.where(upper, full, jnp.flip(full, (0, 1)))
    blocks = jnp.stack([right_side(full[:, k * rows : (k + 1) * rows]) for k in range(count)])
    ordered = jnp.concatenate([lax.dynamic_index_in_dim(blocks, index ^ k, 0, False) for k in range(count)], 0)
    return two_parts(ordered)


def after(value, *others):
    return lax.optimization_barrier((value, *others))[0]


def sweeps(forcing, start, wall_even, wall_odd, diag_shift, band_coef, offsets, pattern, block_inv):
    rows, breadth = start.shape
    points = diag_shift.shape[1]
    bands = band_coef.shape[0]
    width = breadth // points
    chunks = CHUNKS
    n_wall = lax.axis_size("wall")
    sign = jnp.where(lax.axis_index("span") % 2 == 0, 1, -1).astype(jnp.int32)[None]

    raw_first = far(start, True)
    state = list(split(start, chunks, points))
    weights = jnp.swapaxes(band_coef, 1, 2) * pattern.astype(jnp.float32)[:, :, None]
    weights = jnp.concatenate([weights, diag_shift.T[None]], 0).reshape((bands + 1) * points, rows)
    low = weights[:, LANES:]
    own_w = jnp.stack([weights[:, :LANES], jnp.concatenate([low, low], 1)])
    their_w = partner(own_w[:, : bands * points])
    mh, ml = wall_rows(wall_even, wall_odd, rows)
    bh, bl = two_parts(right_side(block_inv))
    f = split(forcing, chunks, points)
    residual = [None] * chunks
    arrived = raw_first
    order = [0]
    bit = n_wall // 2
    while bit:
        order = order + [o ^ bit for o in order]
        bit //= 2
    for sweep in range(SWEEPS):
        final_sweep = sweep == SWEEPS - 1
        if sweep:
            firsts = [far(after(state[k], arrived), True) for k in range(chunks)]
            arrived = firsts[-1]
        else:
            firsts = split(raw_first, chunks, points)
        seconds = [far(after(state[k], arrived), False) for k in range(chunks)]
        arrived = seconds[-1]
        walls = []
        for k in range(chunks):
            got = [state[k]]
            bit = n_wall // 2
            while bit:
                got = got + [exchange(v, bit) for v in got]
                bit //= 2
            walls.append([got[order.index(o)] for o in range(n_wall)])
        theirs = []
        sums = []
        for k in range(chunks):
            partial, own_sum = near(offsets, sign, state[k], firsts[k], own_w, their_w)
            sums.append(own_sum)
            theirs.append(partner(partial))
        new = []
        for k in range(chunks):
            g = wall(f[k], mh, ml, walls[k])
            final = final_sweep and k == chunks - 1
            earlier = [a for pair in new for a in pair] if final else []
            new.append(
                last(
                    offsets,
                    sign,
                    g,
                    sums[k],
                    theirs[k],
                    state[k],
                    seconds[k],
                    own_w,
                    bh,
                    bl,
                    earlier,
                    width if final else 0,
                )
            )
        state = [pair[0] for pair in new]
        residual = [pair[1] for pair in new]
    return state[-1], residual[-1]


def solution(mesh):
    in_specs = (
        P("wall", "span"),
        P("wall", "span"),
        P(),
        P(),
        P("wall", "span"),
        P(None, "wall", "span"),
        P(),
        P(None, "span"),
        P("wall", None),
    )
    out_specs = (P("wall", "span"), P("wall", "span"))
    return jax.shard_map(sweeps, mesh=mesh, in_specs=in_specs, out_specs=out_specs, check_vma=False)
```

```python
import functools

import jax
import jax.numpy as jnp
from jax import lax
from jax.experimental import pallas as pl
from jax.experimental.pallas import tpu as pltpu
from jax.sharding import PartitionSpec as P


SWEEPS = 2
CHUNKS = 2
LANES = 128
HALF = LANES // 2
REACH = 2


def exchange(value, bit):
    count = lax.axis_size("wall")
    return lax.ppermute(value, "wall", [(i, i ^ bit) for i in range(count)])


def partner(value):
    count = lax.axis_size("span")
    return lax.ppermute(value, "span", [(i, i ^ 1) for i in range(count)])


def far(value, first):
    count = lax.axis_size("span")
    pairs = []
    for i in range(count):
        up = (i % 2 == 1) == first
        pairs.append((i, (i + (REACH if up else -REACH)) % count))
    return lax.ppermute(value, "span", pairs)


def params():
    return pltpu.CompilerParams(vmem_limit_bytes=20 << 20)


SMEM = pl.BlockSpec(memory_space=pltpu.SMEM)
VMEM = pl.BlockSpec(memory_space=pltpu.VMEM)


def split_kernel(width, x_ref, *out_refs):
    chunks = len(out_refs)
    cw = width // chunks
    half = cw // 2
    per = LANES // width

    def step(g, _):
        lanes = pl.ds(pl.multiple_of(g * LANES, LANES), LANES)
        top = x_ref[:LANES, lanes].T.reshape(per, width, LANES)
        low = x_ref[LANES:, lanes]
        pair = jnp.concatenate([low, pltpu.roll(low, LANES - half, 1)], 0)
        pair = pair.T.reshape(per, width, LANES)
        here = pl.ds(g * per, per)
        for k, out_ref in enumerate(out_refs):
            out_ref[here, :cw, :] = top[:, k * cw : (k + 1) * cw, :]
            out_ref[here, cw:, :] = pair[:, k * cw : k * cw + half, :]
        return 0

    lax.fori_loop(0, x_ref.shape[1] // LANES, step, 0)


def split(x, chunks, points):
    rows, breadth = x.shape
    width = breadth // points
    cw = width // chunks
    out = jax.ShapeDtypeStruct((points, cw + cw // 2, LANES), x.dtype)
    return pl.pallas_call(
        functools.partial(split_kernel, width),
        out_shape=(out,) * chunks,
        in_specs=[VMEM],
        out_specs=(VMEM,) * chunks,
        compiler_params=params(),
        cost_estimate=pl.CostEstimate(flops=0, bytes_accessed=8 * rows * breadth, transcendentals=0),
        name="split",
    )(x)


def join(width, sol_parts, res_parts, sol_ref, res_ref, begin, end):
    chunks = len(sol_parts)
    cw = width // chunks
    half = cw // 2
    per = LANES // width
    lower = lax.broadcasted_iota(jnp.int32, (half, LANES), 1) < HALF

    def step(g, _):
        lanes = pl.ds(pl.multiple_of(g * LANES, LANES), LANES)
        for out_ref, parts in ((sol_ref, sol_parts), (res_ref, res_parts)):
            rows = [part[g * per + z, :cw, :] for z in range(per) for part in parts]
            out_ref[:LANES, lanes] = jnp.concatenate(rows, 0).T
        rows = []
        for z in range(per):
            for sol, res in zip(sol_parts, res_parts):
                a = sol[g * per + z, cw:, :]
                b = res[g * per + z, cw:, :]
                rows.append(jnp.where(lower, a, pltpu.roll(b, HALF, 1)))
                rows.append(jnp.where(lower, pltpu.roll(a, HALF, 1), b))
        both = jnp.concatenate(rows, 0).T
        sol_ref[LANES:, lanes] = both[:HALF]
        res_ref[LANES:, lanes] = both[HALF:]
        return 0

    lax.fori_loop(begin, end, step, 0, unroll=2)


UNROLL = 4


def fill(ext_ref, pieces, points):
    def step(i, _):
        for slot in range(ext_ref.shape[0] // points):
            here = pl.ds(slot * points + i * UNROLL, UNROLL)
            ext_ref[here] = jnp.zeros((UNROLL, *ext_ref.shape[1:]), jnp.float32)
        return 0

    lax.fori_loop(0, points // UNROLL, step, 0)

    def copy(i, _):
        for ref, slot in pieces:
            ext_ref[pl.ds(slot * points + i * UNROLL, UNROLL)] = ref[pl.ds(i * UNROLL, UNROLL)]
        return 0

    lax.fori_loop(0, points // UNROLL, copy, 0)


def scaled(w_ref, row, value, cw):
    top = w_ref[0, pl.ds(row, 1), :] * value[:cw]
    low = w_ref[1, pl.ds(row, 1), :] * value[cw:]
    return top, low


def near_kernel(bands, off_ref, sign_ref, x_ref, far_ref, w_ref, theirs_ref, partial_ref, sum_ref, ext_ref):
    points, rows, _ = x_ref.shape
    cw = rows * 2 // 3
    sign = sign_ref[0]
    own = jnp.where(sign > 0, REACH, REACH + 1)
    fill(ext_ref, [(x_ref, own), (far_ref, own + 2 * sign)], points)

    for out_ref, weights, shift in ((partial_ref, theirs_ref, sign), (sum_ref, w_ref, 0)):
        starts = [(own + shift) * points + off_ref[b] for b in range(bands)]

        def step(i, _):
            for u in range(UNROLL):
                p = i * UNROLL + u
                if out_ref is sum_ref:
                    top, low = scaled(weights, bands * points + p, x_ref[p], cw)
                else:
                    top, low = None, None
                for b in range(bands):
                    t, l = scaled(weights, b * points + p, ext_ref[starts[b] + p], cw)
                    top, low = (t, l) if top is None else (top + t, low + l)
                out_ref[p, :cw, :] = top
                out_ref[p, cw:, :] = low
            return 0

        lax.fori_loop(0, points // UNROLL, step, 0)


def near(offsets, sign, x, first, w, theirs):
    bands = offsets.shape[0]
    points, rows, _ = x.shape
    out = jax.ShapeDtypeStruct(x.shape, x.dtype)
    return pl.pallas_call(
        functools.partial(near_kernel, bands),
        out_shape=(out, out),
        in_specs=[SMEM, SMEM, VMEM, VMEM, VMEM, VMEM],
        out_specs=(VMEM, VMEM),
        scratch_shapes=[pltpu.VMEM(((2 * REACH + 2) * points, rows, LANES), jnp.float32)],
        compiler_params=params(),
        cost_estimate=pl.CostEstimate(flops=1000000000, bytes_accessed=6 * x.size * 4, transcendentals=0),
        name="near",
    )(offsets, sign, x, first, w, theirs)


def halves(value):
    high = value.astype(jnp.bfloat16)
    low = (value - high.astype(jnp.float32)).astype(jnp.bfloat16)
    return high, low


def product(high, low, w_high, w_low):
    dot = functools.partial(jnp.dot, preferred_element_type=jnp.float32)
    return dot(high, w_high) + (dot(low, w_high) + dot(high, w_low))


def stage(high_ref, low_ref, at, ref, cw):
    points = ref.shape[0]
    half = cw // 2
    count = points * half
    low = ref[:, cw:, :].reshape(count, LANES)
    turned = pltpu.roll(low, HALF, 1)
    for part, top, rest in ((0, ref[:, :half, :], low), (1, ref[:, half:cw, :], turned)):
        rows = slice(part * count, (part + 1) * count)
        for n, value in enumerate((top.reshape(count, LANES), rest)):
            columns = slice(at + n * LANES, at + (n + 1) * LANES)
            high, small = halves(value)
            high_ref[rows, columns] = high
            low_ref[rows, columns] = small


def unstage(value, points, cw):
    half = cw // 2
    count = points * half
    first, second = value[:count], value[count:]
    top = [v[:, :LANES].reshape(points, half, LANES) for v in (first, second)]
    low = first[:, LANES:] + pltpu.roll(second[:, LANES:], HALF, 1)
    return top, low.reshape(points, half, LANES)


def wall_kernel(n_blocks, f_ref, s_ref, mh_ref, ml_ref, *rest):
    blocks = rest[:n_blocks]
    out_ref, high_ref, low_ref = rest[n_blocks:]
    points, rows, _ = f_ref.shape
    cw = rows * 2 // 3
    half = cw // 2
    for k, ref in enumerate(blocks):
        stage(high_ref, low_ref, 2 * LANES * k, ref, cw)
    result = product(high_ref[...], low_ref[...], mh_ref[...], ml_ref[...])
    top, low = unstage(result, points, cw)
    out_ref[:, :half, :] = f_ref[:, :half, :] - s_ref[:, :half, :] - top[0]
    out_ref[:, half:cw, :] = f_ref[:, half:cw, :] - s_ref[:, half:cw, :] - top[1]
    out_ref[:, cw:, :] = f_ref[:, cw:, :] - s_ref[:, cw:, :] - low


def wall(f, s, mh, ml, blocks):
    points, rows, _ = f.shape
    n_blocks = len(blocks)
    m_rows = points * rows * 2 // 3
    return pl.pallas_call(
        functools.partial(wall_kernel, n_blocks),
        out_shape=jax.ShapeDtypeStruct(f.shape, f.dtype),
        in_specs=[VMEM] * (4 + n_blocks),
        out_specs=VMEM,
        scratch_shapes=[pltpu.VMEM((m_rows, 2 * LANES * n_blocks), jnp.bfloat16)] * 2,
        compiler_params=params(),
        cost_estimate=pl.CostEstimate(flops=3000000000, bytes_accessed=8 * f.size * 4, transcendentals=0),
        name="wall",
    )(f, s, mh, ml, *blocks)


def last_kernel(bands, width, n_earlier, off_ref, sign_ref, g_ref, t_ref, x_ref, far_ref, w_ref, bh_ref, bl_ref, *rest):
    earlier = rest[: 2 * n_earlier]
    rest = rest[2 * n_earlier :]
    if width:
        sol_hbm, res_hbm, high_ref, low_ref, x_new_ref, r_ref, sol_ref, res_ref, sems = rest
    else:
        x_new_ref, r_ref, high_ref, low_ref = rest
    points, rows, _ = x_ref.shape
    cw = rows * 2 // 3
    half = cw // 2
    sign = sign_ref[0]

    def begin(i, _):
        here = pl.ds(i * UNROLL, UNROLL)
        r_ref[here] = g_ref[here] - t_ref[here]
        return 0

    lax.fori_loop(0, points // UNROLL, begin, 0)

    def band(b, _):
        shift = off_ref[b] + 2 * sign * points
        first = jnp.maximum(0, -shift)
        count = points - jnp.abs(shift)

        def point(p):
            top, low = scaled(w_ref, b * points + p, far_ref[p + shift], cw)
            r_ref[p, :cw, :] = r_ref[p, :cw, :] - top
            r_ref[p, cw:, :] = r_ref[p, cw:, :] - low

        def several(i, _):
            for u in range(UNROLL):
                point(first + i * UNROLL + u)
            return 0

        def one(i, _):
            point(first + i)
            return 0

        groups = jnp.maximum(count, 0) // UNROLL
        lax.fori_loop(0, groups, several, 0)
        lax.fori_loop(groups * UNROLL, count, one, 0)
        return 0

    lax.fori_loop(0, bands, band, 0)
    stage(high_ref, low_ref, 0, r_ref, cw)
    result = product(high_ref[...], low_ref[...], bh_ref[...], bl_ref[...])
    top, low = unstage(result, points, cw)
    x_new_ref[:, :half, :] = x_ref[:, :half, :] + top[0]
    x_new_ref[:, half:cw, :] = x_ref[:, half:cw, :] + top[1]
    x_new_ref[:, cw:, :] = x_ref[:, cw:, :] + low
    if width:
        slabs = sems.shape[1]
        wide = sol_ref.shape[1] // slabs

        def copies(n):
            at = pl.ds(pl.multiple_of(n * wide, LANES), wide)
            return [
                pltpu.make_async_copy(ref.at[:, at], hbm.at[:, at], sems.at[which, n])
                for which, (ref, hbm) in enumerate(((sol_ref, sol_hbm), (res_ref, res_hbm)))
            ]

        for n in range(slabs):
            join(width, [*earlier[::2], x_new_ref], [*earlier[1::2], r_ref], sol_ref, res_ref, n * wide // LANES, (n + 1) * wide // LANES)
            for copy in copies(n):
                copy.start()
        for n in range(slabs):
            for copy in copies(n):
                copy.wait()


SLABS = 4


def last(offsets, sign, g, t, x, second, w, bh, bl, earlier, width):
    bands = offsets.shape[0]
    points, rows, _ = x.shape
    chunk = pltpu.VMEM(x.shape, jnp.float32)
    shape = (LANES + HALF, points * width) if width else x.shape
    out = jax.ShapeDtypeStruct(shape, x.dtype)
    m_rows = points * rows * 2 // 3
    whole = pltpu.VMEM(shape, jnp.float32)
    return pl.pallas_call(
        functools.partial(last_kernel, bands, width, len(earlier) // 2),
        out_shape=(out, out),
        in_specs=[SMEM, SMEM] + [VMEM] * (7 + len(earlier)),
        out_specs=(pl.BlockSpec(memory_space=pltpu.HBM) if width else VMEM,) * 2,
        scratch_shapes=[
            pltpu.VMEM((m_rows, 2 * LANES), jnp.bfloat16),
            pltpu.VMEM((m_rows, 2 * LANES), jnp.bfloat16),
        ]
        + ([chunk, chunk, whole, whole, pltpu.SemaphoreType.DMA((2, SLABS))] if width else []),
        compiler_params=params(),
        cost_estimate=pl.CostEstimate(flops=1000000000, bytes_accessed=8 * x.size * 4, transcendentals=0),
        name="last",
    )(offsets, sign, g, t, x, second, w, bh, bl, *earlier)


def flip_matrix(rows, turned):
    size = 2 * LANES
    i = lax.broadcasted_iota(jnp.int32, (size, size), 0)
    j = lax.broadcasted_iota(jnp.int32, (size, size), 1)
    target = jnp.where(turned, rows - 1 - i, i)
    return jnp.where(jnp.logical_and(j == target, i < rows), 1.0, 0.0).astype(jnp.bfloat16)


def prep_kernel(count, index_ref, even_ref, odd_ref, inv_ref, mh_ref, ml_ref, bh_ref, bl_ref, pad_ref):
    rows = inv_ref.shape[0]
    size = 2 * LANES
    index = index_ref[0]
    half = count // 2
    lower = index >= half
    at = pl.ds(pl.multiple_of(jnp.where(lower, count - 1 - index, index) * rows, 8), rows)
    pad_ref[...] = jnp.zeros_like(pad_ref)

    def transposed(value):
        pad_ref[:rows, :rows] = value
        return pad_ref[...].T

    high, low = halves(transposed(inv_ref[...]))
    bh_ref[...] = high
    bl_ref[...] = low
    keep_or_turn = flip_matrix(rows, lower)
    turn = flip_matrix(rows, True)
    dot = functools.partial(jnp.dot, preferred_element_type=jnp.float32)
    even = even_ref[at, :]
    odd = odd_ref[at, :]
    for j in range(count):
        block = j if j < half else count - 1 - j
        columns = slice(block * rows, (block + 1) * rows)
        weight = jnp.where(lower == (j >= half), 0.5, -0.5)
        parts = halves(transposed(0.5 * even[:, columns] + weight * odd[:, columns]))
        place = pl.ds(pl.multiple_of(jnp.bitwise_xor(index, j) * size, size), size)
        for out_ref, part in zip((mh_ref, ml_ref), parts):
            if j >= half:
                part = dot(turn, part).astype(jnp.bfloat16)
            out_ref[place, :] = dot(part, keep_or_turn).astype(jnp.bfloat16)


def prep(wall_even, wall_odd, block_inv):
    count = lax.axis_size("wall")
    index = lax.axis_index("wall").astype(jnp.int32)[None]
    size = 2 * LANES
    m = jax.ShapeDtypeStruct((count * size, size), jnp.bfloat16)
    b = jax.ShapeDtypeStruct((size, size), jnp.bfloat16)
    return pl.pallas_call(
        functools.partial(prep_kernel, count),
        out_shape=(m, m, b, b),
        in_specs=[SMEM, VMEM, VMEM, VMEM],
        out_specs=(VMEM,) * 4,
        scratch_shapes=[pltpu.VMEM((size, size), jnp.float32)],
        compiler_params=params(),
        cost_estimate=pl.CostEstimate(flops=600000000, bytes_accessed=3000000, transcendentals=0),
        name="prep",
    )(index, wall_even, wall_odd, block_inv)


def after(value, *others):
    return lax.optimization_barrier((value, *others))[0]


def sweeps(forcing, start, wall_even, wall_odd, diag_shift, band_coef, offsets, pattern, block_inv):
    rows, breadth = start.shape
    points = diag_shift.shape[1]
    bands = band_coef.shape[0]
    width = breadth // points
    chunks = CHUNKS
    n_wall = lax.axis_size("wall")
    sign = jnp.where(lax.axis_index("span") % 2 == 0, 1, -1).astype(jnp.int32)[None]

    raw_first = far(start, True)
    state = list(split(start, chunks, points))
    weights = jnp.swapaxes(band_coef, 1, 2) * pattern.astype(jnp.float32)[:, :, None]
    weights = jnp.concatenate([weights, diag_shift.T[None]], 0).reshape((bands + 1) * points, rows)
    low = weights[:, LANES:]
    own_w = jnp.stack([weights[:, :LANES], jnp.concatenate([low, low], 1)])
    their_w = partner(own_w[:, : bands * points])
    mh, ml, bh, bl = prep(wall_even, wall_odd, block_inv)
    f = split(forcing, chunks, points)
    residual = [None] * chunks
    arrived = raw_first
    order = [0]
    bit = n_wall // 2
    while bit:
        order = order + [o ^ bit for o in order]
        bit //= 2
    for sweep in range(SWEEPS):
        final_sweep = sweep == SWEEPS - 1
        if sweep:
            firsts = [far(after(state[k], arrived), True) for k in range(chunks)]
            arrived = firsts[-1]
        else:
            firsts = split(raw_first, chunks, points)
        seconds = [far(after(state[k], arrived), False) for k in range(chunks)]
        arrived = seconds[-1]
        walls = []
        for k in range(chunks):
            got = [state[k]]
            bit = n_wall // 2
            while bit:
                got = got + [exchange(v, bit) for v in got]
                bit //= 2
            walls.append([got[order.index(o)] for o in range(n_wall)])
        theirs = []
        sums = []
        for k in range(chunks):
            partial, own_sum = near(offsets, sign, state[k], firsts[k], own_w, their_w)
            sums.append(own_sum)
            theirs.append(partner(partial))
        new = []
        for k in range(chunks):
            g = wall(f[k], sums[k], mh, ml, walls[k])
            final = final_sweep and k == chunks - 1
            earlier = [a for pair in new for a in pair] if final else []
            new.append(
                last(offsets, sign, g, theirs[k], state[k], seconds[k], own_w, bh, bl, earlier, width if final else 0)
            )
        state = [pair[0] for pair in new]
        residual = [pair[1] for pair in new]
    return state[-1], residual[-1]


def solution(mesh):
    in_specs = (
        P("wall", "span"),
        P("wall", "span"),
        P(),
        P(),
        P("wall", "span"),
        P(None, "wall", "span"),
        P(),
        P(None, "span"),
        P("wall", None),
    )
    out_specs = (P("wall", "span"), P("wall", "span"))
    return jax.shard_map(sweeps, mesh=mesh, in_specs=in_specs, out_specs=out_specs, check_vma=False)
```

```python
import functools

import jax
import jax.numpy as jnp
from jax import lax
from jax.experimental import pallas as pl
from jax.experimental.pallas import tpu as pltpu
from jax.sharding import PartitionSpec as P


SWEEPS = 2
CHUNKS = 2
LANES = 128
HALF = LANES // 2
REACH = 2


def exchange(value, bit):
    count = lax.axis_size("wall")
    return lax.ppermute(value, "wall", [(i, i ^ bit) for i in range(count)])


def partner(value):
    count = lax.axis_size("span")
    return lax.ppermute(value, "span", [(i, i ^ 1) for i in range(count)])


def far(value, first):
    count = lax.axis_size("span")
    pairs = []
    for i in range(count):
        up = (i % 2 == 1) == first
        pairs.append((i, (i + (REACH if up else -REACH)) % count))
    return lax.ppermute(value, "span", pairs)


def params():
    return pltpu.CompilerParams(vmem_limit_bytes=20 << 20)


SMEM = pl.BlockSpec(memory_space=pltpu.SMEM)
VMEM = pl.BlockSpec(memory_space=pltpu.VMEM)


def split_kernel(width, x_ref, *out_refs):
    chunks = len(out_refs)
    cw = width // chunks
    half = cw // 2
    per = LANES // width

    def step(g, _):
        lanes = pl.ds(pl.multiple_of(g * LANES, LANES), LANES)
        top = x_ref[:LANES, lanes].T.reshape(per, width, LANES)
        low = x_ref[LANES:, lanes]
        pair = jnp.concatenate([low, pltpu.roll(low, LANES - half, 1)], 0)
        pair = pair.T.reshape(per, width, LANES)
        here = pl.ds(g * per, per)
        for k, out_ref in enumerate(out_refs):
            out_ref[here, :cw, :] = top[:, k * cw : (k + 1) * cw, :]
            out_ref[here, cw:, :] = pair[:, k * cw : k * cw + half, :]
        return 0

    lax.fori_loop(0, x_ref.shape[1] // LANES, step, 0)


def split(x, chunks, points):
    rows, breadth = x.shape
    width = breadth // points
    cw = width // chunks
    out = jax.ShapeDtypeStruct((points, cw + cw // 2, LANES), x.dtype)
    return pl.pallas_call(
        functools.partial(split_kernel, width),
        out_shape=(out,) * chunks,
        in_specs=[VMEM],
        out_specs=(VMEM,) * chunks,
        compiler_params=params(),
        cost_estimate=pl.CostEstimate(flops=0, bytes_accessed=8 * rows * breadth, transcendentals=0),
        name="split",
    )(x)


def join(width, sol_parts, res_parts, sol_ref, res_ref, begin, end):
    chunks = len(sol_parts)
    cw = width // chunks
    half = cw // 2
    per = LANES // width
    lower = lax.broadcasted_iota(jnp.int32, (half, LANES), 1) < HALF

    def step(g, _):
        lanes = pl.ds(pl.multiple_of(g * LANES, LANES), LANES)
        for out_ref, parts in ((sol_ref, sol_parts), (res_ref, res_parts)):
            rows = [part[g * per + z, :cw, :] for z in range(per) for part in parts]
            out_ref[:LANES, lanes] = jnp.concatenate(rows, 0).T
        rows = []
        for z in range(per):
            for sol, res in zip(sol_parts, res_parts):
                a = sol[g * per + z, cw:, :]
                b = res[g * per + z, cw:, :]
                rows.append(jnp.where(lower, a, pltpu.roll(b, HALF, 1)))
                rows.append(jnp.where(lower, pltpu.roll(a, HALF, 1), b))
        both = jnp.concatenate(rows, 0).T
        sol_ref[LANES:, lanes] = both[:HALF]
        res_ref[LANES:, lanes] = both[HALF:]
        return 0

    lax.fori_loop(begin, end, step, 0, unroll=2)


UNROLL = 4


def fill(ext_ref, pieces, points):
    def step(i, _):
        for slot in range(ext_ref.shape[0] // points):
            here = pl.ds(slot * points + i * UNROLL, UNROLL)
            ext_ref[here] = jnp.zeros((UNROLL, *ext_ref.shape[1:]), jnp.float32)
        return 0

    lax.fori_loop(0, points // UNROLL, step, 0)

    def copy(i, _):
        for ref, slot in pieces:
            ext_ref[pl.ds(slot * points + i * UNROLL, UNROLL)] = ref[pl.ds(i * UNROLL, UNROLL)]
        return 0

    lax.fori_loop(0, points // UNROLL, copy, 0)


def scaled(w_ref, row, value, cw):
    top = w_ref[0, pl.ds(row, 1), :] * value[:cw]
    low = w_ref[1, pl.ds(row, 1), :] * value[cw:]
    return top, low


def near_kernel(bands, off_ref, sign_ref, x_ref, far_ref, w_ref, theirs_ref, partial_ref, sum_ref, ext_ref):
    points, rows, _ = x_ref.shape
    cw = rows * 2 // 3
    sign = sign_ref[0]
    own = jnp.where(sign > 0, REACH, REACH + 1)
    fill(ext_ref, [(x_ref, own), (far_ref, own + 2 * sign)], points)

    for out_ref, weights, shift in ((partial_ref, theirs_ref, sign), (sum_ref, w_ref, 0)):
        starts = [(own + shift) * points + off_ref[b] for b in range(bands)]

        def step(i, _):
            for u in range(UNROLL):
                p = i * UNROLL + u
                if out_ref is sum_ref:
                    top, low = scaled(weights, bands * points + p, x_ref[p], cw)
                else:
                    top, low = None, None
                for b in range(bands):
                    t, l = scaled(weights, b * points + p, ext_ref[starts[b] + p], cw)
                    top, low = (t, l) if top is None else (top + t, low + l)
                out_ref[p, :cw, :] = top
                out_ref[p, cw:, :] = low
            return 0

        lax.fori_loop(0, points // UNROLL, step, 0)


def near(offsets, sign, x, first, w, theirs):
    bands = offsets.shape[0]
    points, rows, _ = x.shape
    out = jax.ShapeDtypeStruct(x.shape, x.dtype)
    return pl.pallas_call(
        functools.partial(near_kernel, bands),
        out_shape=(out, out),
        in_specs=[SMEM, SMEM, VMEM, VMEM, VMEM, VMEM],
        out_specs=(VMEM, VMEM),
        scratch_shapes=[pltpu.VMEM(((2 * REACH + 2) * points, rows, LANES), jnp.float32)],
        compiler_params=params(),
        cost_estimate=pl.CostEstimate(flops=1000000000, bytes_accessed=6 * x.size * 4, transcendentals=0),
        name="near",
    )(offsets, sign, x, first, w, theirs)


def halves(value):
    high = value.astype(jnp.bfloat16)
    low = (value - high.astype(jnp.float32)).astype(jnp.bfloat16)
    return high, low


def product(high, low, w_high, w_low):
    dot = functools.partial(jnp.dot, preferred_element_type=jnp.float32)
    return dot(high, w_high) + (dot(low, w_high) + dot(high, w_low))


def stage(high_ref, low_ref, at, ref, cw):
    points = ref.shape[0]
    half = cw // 2
    count = points * half
    low = ref[:, cw:, :].reshape(count, LANES)
    turned = pltpu.roll(low, HALF, 1)
    for part, top, rest in ((0, ref[:, :half, :], low), (1, ref[:, half:cw, :], turned)):
        rows = slice(part * count, (part + 1) * count)
        for n, value in enumerate((top.reshape(count, LANES), rest)):
            columns = slice(at + n * LANES, at + (n + 1) * LANES)
            high, small = halves(value)
            high_ref[rows, columns] = high
            low_ref[rows, columns] = small


def unstage(value, points, cw):
    half = cw // 2
    count = points * half
    first, second = value[:count], value[count:]
    top = [v[:, :LANES].reshape(points, half, LANES) for v in (first, second)]
    low = first[:, LANES:] + pltpu.roll(second[:, LANES:], HALF, 1)
    return top, low.reshape(points, half, LANES)


def wall_kernel(n_blocks, f_ref, s_ref, mh_ref, ml_ref, *rest):
    blocks = rest[:n_blocks]
    out_ref, high_ref, low_ref = rest[n_blocks:]
    points, rows, _ = f_ref.shape
    cw = rows * 2 // 3
    half = cw // 2
    for k, ref in enumerate(blocks):
        stage(high_ref, low_ref, 2 * LANES * k, ref, cw)
    result = product(high_ref[...], low_ref[...], mh_ref[...], ml_ref[...])
    top, low = unstage(result, points, cw)
    out_ref[:, :half, :] = f_ref[:, :half, :] - s_ref[:, :half, :] - top[0]
    out_ref[:, half:cw, :] = f_ref[:, half:cw, :] - s_ref[:, half:cw, :] - top[1]
    out_ref[:, cw:, :] = f_ref[:, cw:, :] - s_ref[:, cw:, :] - low


def wall(f, s, mh, ml, blocks):
    points, rows, _ = f.shape
    n_blocks = len(blocks)
    m_rows = points * rows * 2 // 3
    return pl.pallas_call(
        functools.partial(wall_kernel, n_blocks),
        out_shape=jax.ShapeDtypeStruct(f.shape, f.dtype),
        in_specs=[VMEM] * (4 + n_blocks),
        out_specs=VMEM,
        scratch_shapes=[pltpu.VMEM((m_rows, 2 * LANES * n_blocks), jnp.bfloat16)] * 2,
        compiler_params=params(),
        cost_estimate=pl.CostEstimate(flops=3000000000, bytes_accessed=8 * f.size * 4, transcendentals=0),
        name="wall",
    )(f, s, mh, ml, *blocks)


def far_terms(bands, lo, n, sign, off_ref, w_ref, far_ref, r_ref):
    points, rows, _ = far_ref.shape
    cw = rows * 2 // 3

    def band(b, _):
        shift = off_ref[b] + 2 * sign * points
        first = jnp.maximum(lo, -shift)
        count = jnp.minimum(lo + n, points - shift) - first

        def point(p):
            top, low = scaled(w_ref, b * points + p, far_ref[p + shift], cw)
            r_ref[p - lo, :cw, :] = r_ref[p - lo, :cw, :] - top
            r_ref[p - lo, cw:, :] = r_ref[p - lo, cw:, :] - low

        def several(i, _):
            for u in range(UNROLL):
                point(first + i * UNROLL + u)
            return 0

        def one(i, _):
            point(first + i)
            return 0

        groups = jnp.maximum(count, 0) // UNROLL
        lax.fori_loop(0, groups, several, 0)
        lax.fori_loop(groups * UNROLL, count, one, 0)
        return 0

    lax.fori_loop(0, bands, band, 0)


def update(x_ref, lo, r_ref, high_ref, low_ref, bh_ref, bl_ref, x_new_ref):
    n, rows, _ = r_ref.shape
    cw = rows * 2 // 3
    half = cw // 2
    stage(high_ref, low_ref, 0, r_ref, cw)
    result = product(high_ref[...], low_ref[...], bh_ref[...], bl_ref[...])
    top, low = unstage(result, n, cw)
    here = pl.ds(lo, n)
    x_new_ref[:, :half, :] = x_ref[here, :half, :] + top[0]
    x_new_ref[:, half:cw, :] = x_ref[here, half:cw, :] + top[1]
    x_new_ref[:, cw:, :] = x_ref[here, cw:, :] + low


def last_kernel(bands, off_ref, sign_ref, g_ref, t_ref, x_ref, w_ref, bh_ref, bl_ref, far_ref, x_new_ref, r_ref, high_ref, low_ref):
    points = x_ref.shape[0]

    def begin(i, _):
        here = pl.ds(i * UNROLL, UNROLL)
        r_ref[here] = g_ref[here] - t_ref[here]
        return 0

    lax.fori_loop(0, points // UNROLL, begin, 0)
    far_terms(bands, 0, points, sign_ref[0], off_ref, w_ref, far_ref, r_ref)
    update(x_ref, 0, r_ref, high_ref, low_ref, bh_ref, bl_ref, x_new_ref)


def last(offsets, sign, g, t, x, w, bh, bl, second):
    bands = offsets.shape[0]
    points, rows, _ = x.shape
    out = jax.ShapeDtypeStruct(x.shape, x.dtype)
    m_rows = points * rows * 2 // 3
    return pl.pallas_call(
        functools.partial(last_kernel, bands),
        out_shape=(out, out),
        in_specs=[SMEM, SMEM] + [VMEM] * 7,
        out_specs=(VMEM, VMEM),
        scratch_shapes=[pltpu.VMEM((m_rows, 2 * LANES), jnp.bfloat16)] * 2,
        compiler_params=params(),
        cost_estimate=pl.CostEstimate(flops=1000000000, bytes_accessed=8 * x.size * 4, transcendentals=0),
        name="last",
    )(offsets, sign, g, t, x, w, bh, bl, second)


def piece_start(sizes, i, points):
    before = sum(sizes[:i])
    even = lax.rem(lax.axis_index("span"), 2) == 0
    return jnp.where(even, points - before - sizes[i], before)


def finish_kernel(bands, width, sizes, i, off_ref, g_ref, t_ref, x_ref, w_ref, bh_ref, bl_ref, *rest):
    fars = rest[: i + 1]
    n_outs = 2 if i else 0
    *earlier, sol_hbm, res_hbm, far_ref, high_ref, low_ref, x_new_ref, r_ref, sol_ref, res_ref, sems = rest[i + 1 :]
    if i:
        earlier = earlier[:-n_outs]
    points = x_ref.shape[0]
    n = sizes[i]
    sign = 1 - 2 * lax.rem(lax.axis_index("span"), 2)
    lo = piece_start(sizes, i, points)
    for m, ref in enumerate(fars):
        at = piece_start(sizes, m, points)

        def copy(j, _):
            far_ref[pl.ds(at + j * UNROLL, UNROLL)] = ref[pl.ds(j * UNROLL, UNROLL)]
            return 0

        lax.fori_loop(0, sizes[m] // UNROLL, copy, 0)

    def begin(j, _):
        here = pl.ds(lo + j * UNROLL, UNROLL)
        r_ref[pl.ds(j * UNROLL, UNROLL)] = g_ref[here] - t_ref[here]
        return 0

    lax.fori_loop(0, n // UNROLL, begin, 0)
    far_terms(bands, lo, n, sign, off_ref, w_ref, far_ref, r_ref)
    update(x_ref, lo, r_ref, high_ref, low_ref, bh_ref, bl_ref, x_new_ref)
    views = [ref.at[pl.ds(lo, n)] for ref in earlier]
    slabs = sems.shape[1]
    wide = n * width // slabs
    copies = []
    for m in range(slabs):
        join(width, [*views[::2], x_new_ref], [*views[1::2], r_ref], sol_ref, res_ref, m * wide // LANES, (m + 1) * wide // LANES)
        here = pl.ds(m * wide, wide)
        there = pl.ds(pl.multiple_of(lo * width + m * wide, LANES), wide)
        for which, (ref, hbm) in enumerate(((sol_ref, sol_hbm), (res_ref, res_hbm))):
            copy = pltpu.make_async_copy(ref.at[:, here], hbm.at[:, there], sems.at[which, m])
            copy.start()
            copies.append(copy)
    for copy in copies:
        copy.wait()


SLABS = 2


def finish(offsets, g, t, x, w, bh, bl, fars, earlier, outs, sizes, i, width):
    bands = offsets.shape[0]
    points, rows, _ = x.shape
    n = sizes[i]
    piece = pltpu.VMEM((n, rows, LANES), jnp.float32)
    out = jax.ShapeDtypeStruct((LANES + HALF, points * width), x.dtype)
    m_rows = n * rows * 2 // 3
    slab = pltpu.VMEM((LANES + HALF, n * width), jnp.float32)
    hbm = pl.BlockSpec(memory_space=pltpu.HBM)
    inputs = (offsets, g, t, x, w, bh, bl, *fars, *earlier)
    return pl.pallas_call(
        functools.partial(finish_kernel, bands, width, sizes, i),
        out_shape=(out, out),
        in_specs=[SMEM] + [VMEM] * (len(inputs) - 1) + [hbm] * len(outs),
        out_specs=(hbm, hbm),
        input_output_aliases={len(inputs) + k: k for k in range(len(outs))},
        scratch_shapes=[
            pltpu.VMEM(x.shape, jnp.float32),
            pltpu.VMEM((m_rows, 2 * LANES), jnp.bfloat16),
            pltpu.VMEM((m_rows, 2 * LANES), jnp.bfloat16),
            piece,
            piece,
            slab,
            slab,
            pltpu.SemaphoreType.DMA((2, SLABS)),
        ],
        compiler_params=params(),
        cost_estimate=pl.CostEstimate(flops=1000000000, bytes_accessed=8 * x.size * 4, transcendentals=0),
        name="finish",
    )(*inputs, *outs)


def flip_matrix(rows, turned):
    size = 2 * LANES
    i = lax.broadcasted_iota(jnp.int32, (size, size), 0)
    j = lax.broadcasted_iota(jnp.int32, (size, size), 1)
    target = jnp.where(turned, rows - 1 - i, i)
    return jnp.where(jnp.logical_and(j == target, i < rows), 1.0, 0.0).astype(jnp.bfloat16)


def prep_kernel(count, index_ref, even_ref, odd_ref, inv_ref, mh_ref, ml_ref, bh_ref, bl_ref, pad_ref):
    rows = inv_ref.shape[0]
    size = 2 * LANES
    index = index_ref[0]
    half = count // 2
    lower = index >= half
    at = pl.ds(pl.multiple_of(jnp.where(lower, count - 1 - index, index) * rows, 8), rows)
    pad_ref[...] = jnp.zeros_like(pad_ref)

    def transposed(value):
        pad_ref[:rows, :rows] = value
        return pad_ref[...].T

    high, low = halves(transposed(inv_ref[...]))
    bh_ref[...] = high
    bl_ref[...] = low
    keep_or_turn = flip_matrix(rows, lower)
    turn = flip_matrix(rows, True)
    dot = functools.partial(jnp.dot, preferred_element_type=jnp.float32)
    even = even_ref[at, :]
    odd = odd_ref[at, :]
    for j in range(count):
        block = j if j < half else count - 1 - j
        columns = slice(block * rows, (block + 1) * rows)
        weight = jnp.where(lower == (j >= half), 0.5, -0.5)
        parts = halves(transposed(0.5 * even[:, columns] + weight * odd[:, columns]))
        place = pl.ds(pl.multiple_of(jnp.bitwise_xor(index, j) * size, size), size)
        for out_ref, part in zip((mh_ref, ml_ref), parts):
            if j >= half:
                part = dot(turn, part).astype(jnp.bfloat16)
            out_ref[place, :] = dot(part, keep_or_turn).astype(jnp.bfloat16)


def prep(wall_even, wall_odd, block_inv):
    count = lax.axis_size("wall")
    index = lax.axis_index("wall").astype(jnp.int32)[None]
    size = 2 * LANES
    m = jax.ShapeDtypeStruct((count * size, size), jnp.bfloat16)
    b = jax.ShapeDtypeStruct((size, size), jnp.bfloat16)
    return pl.pallas_call(
        functools.partial(prep_kernel, count),
        out_shape=(m, m, b, b),
        in_specs=[SMEM, VMEM, VMEM, VMEM],
        out_specs=(VMEM,) * 4,
        scratch_shapes=[pltpu.VMEM((size, size), jnp.float32)],
        compiler_params=params(),
        cost_estimate=pl.CostEstimate(flops=600000000, bytes_accessed=3000000, transcendentals=0),
        name="prep",
    )(index, wall_even, wall_odd, block_inv)


def after(value, *others):
    return lax.optimization_barrier((value, *others))[0]


def sweeps(forcing, start, wall_even, wall_odd, diag_shift, band_coef, offsets, pattern, block_inv):
    rows, breadth = start.shape
    points = diag_shift.shape[1]
    bands = band_coef.shape[0]
    width = breadth // points
    chunks = CHUNKS
    n_wall = lax.axis_size("wall")
    sign = jnp.where(lax.axis_index("span") % 2 == 0, 1, -1).astype(jnp.int32)[None]

    raw_first = far(start, True)
    state = list(split(start, chunks, points))
    weights = jnp.swapaxes(band_coef, 1, 2) * pattern.astype(jnp.float32)[:, :, None]
    weights = jnp.concatenate([weights, diag_shift.T[None]], 0).reshape((bands + 1) * points, rows)
    low = weights[:, LANES:]
    own_w = jnp.stack([weights[:, :LANES], jnp.concatenate([low, low], 1)])
    their_w = partner(own_w[:, : bands * points])
    mh, ml, bh, bl = prep(wall_even, wall_odd, block_inv)
    f = split(forcing, chunks, points)
    sizes = (points - points // 4, points // 4)
    arrived = raw_first
    order = [0]
    bit = n_wall // 2
    while bit:
        order = order + [o ^ bit for o in order]
        bit //= 2
    for sweep in range(SWEEPS):
        final_sweep = sweep == SWEEPS - 1
        if sweep:
            firsts = [far(after(state[k], arrived), True) for k in range(chunks)]
            arrived = firsts[-1]
        else:
            firsts = split(raw_first, chunks, points)
        seconds = []
        for k in range(chunks):
            value = after(state[k], arrived)
            if final_sweep and k == chunks - 1:
                parts = [lax.dynamic_slice_in_dim(value, piece_start(sizes, i, points), n, 0) for i, n in enumerate(sizes)]
                seconds.append([far(v, False) for v in parts])
            else:
                seconds.append(far(value, False))
        arrived = seconds[-1]
        walls = []
        for k in range(chunks):
            got = [state[k]]
            bit = n_wall // 2
            while bit:
                got = got + [exchange(v, bit) for v in got]
                bit //= 2
            walls.append([got[order.index(o)] for o in range(n_wall)])
        theirs = []
        sums = []
        for k in range(chunks):
            partial, own_sum = near(offsets, sign, state[k], firsts[k], own_w, their_w)
            sums.append(own_sum)
            theirs.append(partner(partial))
        new = []
        for k in range(chunks):
            g = wall(f[k], sums[k], mh, ml, walls[k])
            if final_sweep and k == chunks - 1:
                earlier = [a for pair in new for a in pair]
                outs = ()
                for i in range(len(sizes)):
                    call = functools.partial(finish, sizes=sizes, i=i, width=width)
                    fars = seconds[k][: i + 1]
                    outs = call(offsets, g, theirs[k], state[k], own_w, bh, bl, fars, earlier, outs)
                return outs
            new.append(last(offsets, sign, g, theirs[k], state[k], own_w, bh, bl, seconds[k]))
        state = [pair[0] for pair in new]


def solution(mesh):
    in_specs = (
        P("wall", "span"),
        P("wall", "span"),
        P(),
        P(),
        P("wall", "span"),
        P(None, "wall", "span"),
        P(),
        P(None, "span"),
        P("wall", None),
    )
    out_specs = (P("wall", "span"), P("wall", "span"))
    return jax.shard_map(sweeps, mesh=mesh, in_specs=in_specs, out_specs=out_specs, check_vma=False)
```

```python
import functools

import jax
import jax.numpy as jnp
from jax import lax
from jax.experimental import pallas as pl
from jax.experimental.pallas import tpu as pltpu
from jax.sharding import PartitionSpec as P


SWEEPS = 2
CHUNKS = 2
LANES = 128
HALF = LANES // 2
REACH = 2


def exchange(value, bit):
    count = lax.axis_size("wall")
    return lax.ppermute(value, "wall", [(i, i ^ bit) for i in range(count)])


def partner(value):
    count = lax.axis_size("span")
    return lax.ppermute(value, "span", [(i, i ^ 1) for i in range(count)])


def far(value, first):
    count = lax.axis_size("span")
    pairs = []
    for i in range(count):
        up = (i % 2 == 1) == first
        pairs.append((i, (i + (REACH if up else -REACH)) % count))
    return lax.ppermute(value, "span", pairs)


def params():
    return pltpu.CompilerParams(vmem_limit_bytes=20 << 20)


SMEM = pl.BlockSpec(memory_space=pltpu.SMEM)
VMEM = pl.BlockSpec(memory_space=pltpu.VMEM)


def split_kernel(width, x_ref, *out_refs):
    chunks = len(out_refs)
    cw = width // chunks
    half = cw // 2
    per = LANES // width
    lower = lax.broadcasted_iota(jnp.int32, (half, LANES), 1) < HALF

    def step(g, _):
        lows = []
        for u in range(2):
            lanes = pl.ds(pl.multiple_of((2 * g + u) * LANES, LANES), LANES)
            top = x_ref[:LANES, lanes].T.reshape(per, width, LANES)
            for k, out_ref in enumerate(out_refs):
                out_ref[pl.ds((2 * g + u) * per, per), :cw, :] = top[:, k * cw : (k + 1) * cw, :]
            lows.append(x_ref[LANES:, lanes])
        pair = jnp.concatenate(lows, 0).T
        for z in range(per):
            for k, out_ref in enumerate(out_refs):
                row = z * width + k * cw
                first, second = pair[row : row + half], pair[row + half : row + cw]
                out_ref[2 * g * per + z, cw:, :] = jnp.where(lower, first, pltpu.roll(second, HALF, 1))
                out_ref[(2 * g + 1) * per + z, cw:, :] = jnp.where(lower, pltpu.roll(first, HALF, 1), second)
        return 0

    lax.fori_loop(0, x_ref.shape[1] // (2 * LANES), step, 0, unroll=2)


def split(x, chunks, points):
    rows, breadth = x.shape
    width = breadth // points
    cw = width // chunks
    out = jax.ShapeDtypeStruct((points, cw + cw // 2, LANES), x.dtype)
    return pl.pallas_call(
        functools.partial(split_kernel, width),
        out_shape=(out,) * chunks,
        in_specs=[VMEM],
        out_specs=(VMEM,) * chunks,
        compiler_params=params(),
        cost_estimate=pl.CostEstimate(flops=0, bytes_accessed=8 * rows * breadth, transcendentals=0),
        name="split",
    )(x)


def join_top(width, parts, out_ref, begin, end):
    cw = width // len(parts)
    per = LANES // width
    for g in range(begin, end):
        rows = [part[g * per + z, :cw, :] for z in range(per) for part in parts]
        out_ref[:LANES, g * LANES : (g + 1) * LANES] = jnp.concatenate(rows, 0).T


def join_low(width, sol_parts, res_parts, sol_ref, res_ref, begin, end):
    cw = width // len(sol_parts)
    half = cw // 2
    per = LANES // width
    lower = lax.broadcasted_iota(jnp.int32, (half, LANES), 1) < HALF
    for g in range(begin, end):
        rows = []
        for z in range(per):
            for sol, res in zip(sol_parts, res_parts):
                a = sol[g * per + z, cw:, :]
                b = res[g * per + z, cw:, :]
                rows.append(jnp.where(lower, a, pltpu.roll(b, HALF, 1)))
                rows.append(jnp.where(lower, pltpu.roll(a, HALF, 1), b))
        both = jnp.concatenate(rows, 0).T
        lanes = slice(g * LANES, (g + 1) * LANES)
        sol_ref[LANES:, lanes] = both[:HALF]
        res_ref[LANES:, lanes] = both[HALF:]


def own_sign():
    return 1 - 2 * lax.rem(lax.axis_index("span"), 2)


def read(off_ref):
    value = off_ref[...]
    return [value[b, 0] for b in range(value.shape[0])]


UNROLL = 4


def fill(ext_ref, pieces, points):
    def step(i, _):
        for slot in range(ext_ref.shape[0] // points):
            here = pl.ds(slot * points + i * UNROLL, UNROLL)
            ext_ref[here] = jnp.zeros((UNROLL, *ext_ref.shape[1:]), jnp.float32)
        return 0

    lax.fori_loop(0, points // UNROLL, step, 0)

    def copy(i, _):
        for ref, slot in pieces:
            ext_ref[pl.ds(slot * points + i * UNROLL, UNROLL)] = ref[pl.ds(i * UNROLL, UNROLL)]
        return 0

    lax.fori_loop(0, points // UNROLL, copy, 0)


def scaled(w_ref, row, value, cw):
    top = w_ref[0, pl.ds(row, 1), :] * value[:cw]
    low = w_ref[1, pl.ds(row, 1), :] * value[cw:]
    return top, low


def near_kernel(bands, off_ref, x_ref, far_ref, w_ref, theirs_ref, partial_ref, sum_ref, ext_ref):
    points, rows, _ = x_ref.shape
    cw = rows * 2 // 3
    sign = own_sign()
    offsets = read(off_ref)
    own = jnp.where(sign > 0, REACH, REACH + 1)
    fill(ext_ref, [(x_ref, own), (far_ref, own + 2 * sign)], points)

    for out_ref, weights, shift in ((partial_ref, theirs_ref, sign), (sum_ref, w_ref, 0)):
        starts = [(own + shift) * points + offsets[b] for b in range(bands)]

        def step(i, _):
            for u in range(UNROLL):
                p = i * UNROLL + u
                if out_ref is sum_ref:
                    top, low = scaled(weights, bands * points + p, x_ref[p], cw)
                else:
                    top, low = None, None
                for b in range(bands):
                    t, l = scaled(weights, b * points + p, ext_ref[starts[b] + p], cw)
                    top, low = (t, l) if top is None else (top + t, low + l)
                out_ref[p, :cw, :] = top
                out_ref[p, cw:, :] = low
            return 0

        lax.fori_loop(0, points // UNROLL, step, 0)


def near(offsets, x, first, w, theirs):
    bands = offsets.shape[0]
    points, rows, _ = x.shape
    out = jax.ShapeDtypeStruct(x.shape, x.dtype)
    return pl.pallas_call(
        functools.partial(near_kernel, bands),
        out_shape=(out, out),
        in_specs=[VMEM] * 5,
        out_specs=(VMEM, VMEM),
        scratch_shapes=[pltpu.VMEM(((2 * REACH + 2) * points, rows, LANES), jnp.float32)],
        compiler_params=params(),
        cost_estimate=pl.CostEstimate(flops=1000000000, bytes_accessed=6 * x.size * 4, transcendentals=0),
        name="near",
    )(offsets, x, first, w, theirs)


def halves(value):
    high = value.astype(jnp.bfloat16)
    low = (value - high.astype(jnp.float32)).astype(jnp.bfloat16)
    return high, low


def product(high, low, w_high, w_low):
    dot = functools.partial(jnp.dot, preferred_element_type=jnp.float32)
    return dot(high, w_high) + (dot(low, w_high) + dot(high, w_low))


def stage(high_ref, low_ref, at, ref, cw):
    points = ref.shape[0]
    half = cw // 2
    count = points * half
    low = ref[:, cw:, :].reshape(count, LANES)
    turned = pltpu.roll(low, HALF, 1)
    for part, top, rest in ((0, ref[:, :half, :], low), (1, ref[:, half:cw, :], turned)):
        rows = slice(part * count, (part + 1) * count)
        for n, value in enumerate((top.reshape(count, LANES), rest)):
            columns = slice(at + n * LANES, at + (n + 1) * LANES)
            high, small = halves(value)
            high_ref[rows, columns] = high
            low_ref[rows, columns] = small


def unstage(value, points, cw):
    half = cw // 2
    count = points * half
    first, second = value[:count], value[count:]
    top = [v[:, :LANES].reshape(points, half, LANES) for v in (first, second)]
    low = first[:, LANES:] + pltpu.roll(second[:, LANES:], HALF, 1)
    return top, low.reshape(points, half, LANES)


def wall_kernel(n_blocks, f_ref, s_ref, mh_ref, ml_ref, *rest):
    blocks = rest[:n_blocks]
    out_ref, high_ref, low_ref = rest[n_blocks:]
    points, rows, _ = f_ref.shape
    cw = rows * 2 // 3
    half = cw // 2
    for k, ref in enumerate(blocks):
        stage(high_ref, low_ref, 2 * LANES * k, ref, cw)
    result = product(high_ref[...], low_ref[...], mh_ref[...], ml_ref[...])
    top, low = unstage(result, points, cw)
    out_ref[:, :half, :] = f_ref[:, :half, :] - s_ref[:, :half, :] - top[0]
    out_ref[:, half:cw, :] = f_ref[:, half:cw, :] - s_ref[:, half:cw, :] - top[1]
    out_ref[:, cw:, :] = f_ref[:, cw:, :] - s_ref[:, cw:, :] - low


def wall(f, s, mh, ml, blocks):
    points, rows, _ = f.shape
    n_blocks = len(blocks)
    m_rows = points * rows * 2 // 3
    return pl.pallas_call(
        functools.partial(wall_kernel, n_blocks),
        out_shape=jax.ShapeDtypeStruct(f.shape, f.dtype),
        in_specs=[VMEM] * (4 + n_blocks),
        out_specs=VMEM,
        scratch_shapes=[pltpu.VMEM((m_rows, 2 * LANES * n_blocks), jnp.bfloat16)] * 2,
        compiler_params=params(),
        cost_estimate=pl.CostEstimate(flops=3000000000, bytes_accessed=8 * f.size * 4, transcendentals=0),
        name="wall",
    )(f, s, mh, ml, *blocks)


def far_terms(lo, n, off_ref, w_ref, far_ref, r_ref):
    points, rows, _ = far_ref.shape
    cw = rows * 2 // 3

    sign = own_sign()
    for b, offset in enumerate(read(off_ref)):
        shift = offset + 2 * sign * points
        first = jnp.maximum(lo, -shift)
        count = jnp.minimum(lo + n, points - shift) - first

        def point(p, b=b, shift=shift):
            top, low = scaled(w_ref, b * points + p, far_ref[p + shift], cw)
            r_ref[p - lo, :cw, :] = r_ref[p - lo, :cw, :] - top
            r_ref[p - lo, cw:, :] = r_ref[p - lo, cw:, :] - low

        def several(i, _, first=first, point=point):
            for u in range(UNROLL):
                point(first + i * UNROLL + u)
            return 0

        def one(i, _, first=first, point=point):
            point(first + i)
            return 0

        groups = jnp.maximum(count, 0) // UNROLL
        lax.fori_loop(0, groups, several, 0)
        lax.fori_loop(groups * UNROLL, count, one, 0)


def update(x_ref, lo, r_ref, high_ref, low_ref, bh_ref, bl_ref, x_new_ref):
    n, rows, _ = r_ref.shape
    cw = rows * 2 // 3
    half = cw // 2
    stage(high_ref, low_ref, 0, r_ref, cw)
    result = product(high_ref[...], low_ref[...], bh_ref[...], bl_ref[...])
    top, low = unstage(result, n, cw)
    here = pl.ds(lo, n)
    x_new_ref[:, :half, :] = x_ref[here, :half, :] + top[0]
    x_new_ref[:, half:cw, :] = x_ref[here, half:cw, :] + top[1]
    x_new_ref[:, cw:, :] = x_ref[here, cw:, :] + low


def last_kernel(off_ref, g_ref, t_ref, x_ref, w_ref, bh_ref, bl_ref, far_ref, x_new_ref, r_ref, high_ref, low_ref):
    points = x_ref.shape[0]

    def begin(i, _):
        here = pl.ds(i * UNROLL, UNROLL)
        r_ref[here] = g_ref[here] - t_ref[here]
        return 0

    lax.fori_loop(0, points // UNROLL, begin, 0)
    far_terms(0, points, off_ref, w_ref, far_ref, r_ref)
    update(x_ref, 0, r_ref, high_ref, low_ref, bh_ref, bl_ref, x_new_ref)


def last(offsets, g, t, x, w, bh, bl, second):
    points, rows, _ = x.shape
    out = jax.ShapeDtypeStruct(x.shape, x.dtype)
    m_rows = points * rows * 2 // 3
    return pl.pallas_call(
        last_kernel,
        out_shape=(out, out),
        in_specs=[VMEM] * 8,
        out_specs=(VMEM, VMEM),
        scratch_shapes=[pltpu.VMEM((m_rows, 2 * LANES), jnp.bfloat16)] * 2,
        compiler_params=params(),
        cost_estimate=pl.CostEstimate(flops=1000000000, bytes_accessed=8 * x.size * 4, transcendentals=0),
        name="last",
    )(offsets, g, t, x, w, bh, bl, second)


def piece_start(sizes, i, points):
    before = sum(sizes[:i])
    even = lax.rem(lax.axis_index("span"), 2) == 0
    return jnp.where(even, points - before - sizes[i], before)


def finish_kernel(width, sizes, i, off_ref, g_ref, t_ref, x_ref, w_ref, bh_ref, bl_ref, *rest):
    fars = rest[: i + 1]
    n_outs = 2 if i else 0
    *earlier, sol_hbm, res_hbm, far_ref, high_ref, low_ref, x_new_ref, r_ref, sol_ref, res_ref, sems = rest[i + 1 :]
    if i:
        earlier = earlier[:-n_outs]
    points = x_ref.shape[0]
    n = sizes[i]
    lo = piece_start(sizes, i, points)
    for m, ref in enumerate(fars):
        at = piece_start(sizes, m, points)

        def copy(j, _):
            far_ref[pl.ds(at + j * UNROLL, UNROLL)] = ref[pl.ds(j * UNROLL, UNROLL)]
            return 0

        lax.fori_loop(0, sizes[m] // UNROLL, copy, 0)

    def begin(j, _):
        here = pl.ds(lo + j * UNROLL, UNROLL)
        r_ref[pl.ds(j * UNROLL, UNROLL)] = g_ref[here] - t_ref[here]
        return 0

    lax.fori_loop(0, n // UNROLL, begin, 0)
    far_terms(lo, n, off_ref, w_ref, far_ref, r_ref)
    views = [ref.at[pl.ds(lo, n)] for ref in earlier]
    sols, ress = [*views[::2], x_new_ref], [*views[1::2], r_ref]
    vectors = n * width // LANES
    join_top(width, ress, res_ref, 0, vectors)
    update(x_ref, lo, r_ref, high_ref, low_ref, bh_ref, bl_ref, x_new_ref)
    slabs = sems.shape[1]
    each = vectors // slabs
    copies = []
    for m in range(slabs):
        join_top(width, sols, sol_ref, m * each, (m + 1) * each)
        join_low(width, sols, ress, sol_ref, res_ref, m * each, (m + 1) * each)
        here = pl.ds(m * each * LANES, each * LANES)
        there = pl.ds(pl.multiple_of(lo * width + m * each * LANES, LANES), each * LANES)
        for which, (ref, hbm) in enumerate(((sol_ref, sol_hbm), (res_ref, res_hbm))):
            copy = pltpu.make_async_copy(ref.at[:, here], hbm.at[:, there], sems.at[which, m])
            copy.start()
            copies.append(copy)
    for copy in copies:
        copy.wait()


SLABS = 2


def finish(offsets, g, t, x, w, bh, bl, fars, earlier, outs, sizes, i, width):
    points, rows, _ = x.shape
    n = sizes[i]
    piece = pltpu.VMEM((n, rows, LANES), jnp.float32)
    out = jax.ShapeDtypeStruct((LANES + HALF, points * width), x.dtype)
    m_rows = n * rows * 2 // 3
    slab = pltpu.VMEM((LANES + HALF, n * width), jnp.float32)
    hbm = pl.BlockSpec(memory_space=pltpu.HBM)
    inputs = (offsets, g, t, x, w, bh, bl, *fars, *earlier)
    return pl.pallas_call(
        functools.partial(finish_kernel, width, sizes, i),
        out_shape=(out, out),
        in_specs=[VMEM] * len(inputs) + [hbm] * len(outs),
        out_specs=(hbm, hbm),
        input_output_aliases={len(inputs) + k: k for k in range(len(outs))},
        scratch_shapes=[
            pltpu.VMEM(x.shape, jnp.float32),
            pltpu.VMEM((m_rows, 2 * LANES), jnp.bfloat16),
            pltpu.VMEM((m_rows, 2 * LANES), jnp.bfloat16),
            piece,
            piece,
            slab,
            slab,
            pltpu.SemaphoreType.DMA((2, SLABS)),
        ],
        compiler_params=params(),
        cost_estimate=pl.CostEstimate(flops=1000000000, bytes_accessed=8 * x.size * 4, transcendentals=0),
        name="finish",
    )(*inputs, *outs)


def flip_matrix(rows, turned):
    size = 2 * LANES
    i = lax.broadcasted_iota(jnp.int32, (size, size), 0)
    j = lax.broadcasted_iota(jnp.int32, (size, size), 1)
    target = jnp.where(turned, rows - 1 - i, i)
    return jnp.where(jnp.logical_and(j == target, i < rows), 1.0, 0.0).astype(jnp.bfloat16)


def prep_kernel(count, index_ref, even_ref, odd_ref, inv_ref, mh_ref, ml_ref, bh_ref, bl_ref, pad_ref):
    rows = inv_ref.shape[0]
    size = 2 * LANES
    index = index_ref[0]
    half = count // 2
    lower = index >= half
    at = pl.ds(pl.multiple_of(jnp.where(lower, count - 1 - index, index) * rows, 8), rows)
    pad_ref[...] = jnp.zeros_like(pad_ref)

    def transposed(value):
        pad_ref[:rows, :rows] = value
        return pad_ref[...].T

    high, low = halves(transposed(inv_ref[...]))
    bh_ref[...] = high
    bl_ref[...] = low
    keep_or_turn = flip_matrix(rows, lower)
    turn = flip_matrix(rows, True)
    dot = functools.partial(jnp.dot, preferred_element_type=jnp.float32)
    even = even_ref[at, :]
    odd = odd_ref[at, :]
    for j in range(count):
        block = j if j < half else count - 1 - j
        columns = slice(block * rows, (block + 1) * rows)
        weight = jnp.where(lower == (j >= half), 0.5, -0.5)
        parts = halves(transposed(0.5 * even[:, columns] + weight * odd[:, columns]))
        place = pl.ds(pl.multiple_of(jnp.bitwise_xor(index, j) * size, size), size)
        for out_ref, part in zip((mh_ref, ml_ref), parts):
            if j >= half:
                part = dot(turn, part).astype(jnp.bfloat16)
            out_ref[place, :] = dot(part, keep_or_turn).astype(jnp.bfloat16)


def prep(wall_even, wall_odd, block_inv):
    count = lax.axis_size("wall")
    index = lax.axis_index("wall").astype(jnp.int32)[None]
    size = 2 * LANES
    m = jax.ShapeDtypeStruct((count * size, size), jnp.bfloat16)
    b = jax.ShapeDtypeStruct((size, size), jnp.bfloat16)
    return pl.pallas_call(
        functools.partial(prep_kernel, count),
        out_shape=(m, m, b, b),
        in_specs=[SMEM, VMEM, VMEM, VMEM],
        out_specs=(VMEM,) * 4,
        scratch_shapes=[pltpu.VMEM((size, size), jnp.float32)],
        compiler_params=params(),
        cost_estimate=pl.CostEstimate(flops=600000000, bytes_accessed=3000000, transcendentals=0),
        name="prep",
    )(index, wall_even, wall_odd, block_inv)


def after(value, *others):
    return lax.optimization_barrier((value, *others))[0]


def sweeps(forcing, start, wall_even, wall_odd, diag_shift, band_coef, offsets, pattern, block_inv):
    rows, breadth = start.shape
    points = diag_shift.shape[1]
    bands = band_coef.shape[0]
    width = breadth // points
    chunks = CHUNKS
    n_wall = lax.axis_size("wall")
    offsets = jnp.broadcast_to(offsets[:, None], (bands, LANES))

    raw_first = far(start, True)
    state = list(split(start, chunks, points))
    weights = jnp.swapaxes(band_coef, 1, 2) * pattern.astype(jnp.float32)[:, :, None]
    weights = jnp.concatenate([weights, diag_shift.T[None]], 0).reshape((bands + 1) * points, rows)
    low = weights[:, LANES:]
    own_w = jnp.stack([weights[:, :LANES], jnp.concatenate([low, low], 1)])
    their_w = partner(own_w[:, : bands * points])
    mh, ml, bh, bl = prep(wall_even, wall_odd, block_inv)
    f = split(forcing, chunks, points)
    sizes = (points * 5 // 8, points * 3 // 8)
    arrived = raw_first
    order = [0]
    bit = n_wall // 2
    while bit:
        order = order + [o ^ bit for o in order]
        bit //= 2
    for sweep in range(SWEEPS):
        final_sweep = sweep == SWEEPS - 1
        if sweep:
            firsts = [far(after(state[k], arrived), True) for k in range(chunks)]
            arrived = firsts[-1]
        else:
            firsts = split(raw_first, chunks, points)
        seconds = []
        for k in range(chunks):
            value = after(state[k], arrived)
            if final_sweep and k == chunks - 1:
                parts = [lax.dynamic_slice_in_dim(value, piece_start(sizes, i, points), n, 0) for i, n in enumerate(sizes)]
                seconds.append([far(v, False) for v in parts])
            else:
                seconds.append(far(value, False))
        arrived = seconds[-1]
        walls = []
        for k in range(chunks):
            got = [state[k]]
            bit = n_wall // 2
            while bit:
                got = got + [exchange(v, bit) for v in got]
                bit //= 2
            walls.append([got[order.index(o)] for o in range(n_wall)])
        theirs = []
        sums = []
        for k in range(chunks):
            partial, own_sum = near(offsets, state[k], firsts[k], own_w, their_w)
            sums.append(own_sum)
            theirs.append(partner(partial))
        new = []
        for k in range(chunks):
            g = wall(f[k], sums[k], mh, ml, walls[k])
            if final_sweep and k == chunks - 1:
                earlier = [a for pair in new for a in pair]
                outs = ()
                for i in range(len(sizes)):
                    call = functools.partial(finish, sizes=sizes, i=i, width=width)
                    fars = seconds[k][: i + 1]
                    outs = call(offsets, g, theirs[k], state[k], own_w, bh, bl, fars, earlier, outs)
                return outs
            new.append(last(offsets, g, theirs[k], state[k], own_w, bh, bl, seconds[k]))
        state = [pair[0] for pair in new]


def solution(mesh):
    in_specs = (
        P("wall", "span"),
        P("wall", "span"),
        P(),
        P(),
        P("wall", "span"),
        P(None, "wall", "span"),
        P(),
        P(None, "span"),
        P("wall", None),
    )
    out_specs = (P("wall", "span"), P("wall", "span"))
    return jax.shard_map(sweeps, mesh=mesh, in_specs=in_specs, out_specs=out_specs, check_vma=False)
```

```python
import functools

import jax
import jax.numpy as jnp
from jax import lax
from jax.experimental import pallas as pl
from jax.experimental.pallas import tpu as pltpu
from jax.sharding import PartitionSpec as P


SWEEPS = 2
CHUNKS = 2
LANES = 128
HALF = LANES // 2
REACH = 2


def exchange(value, bit):
    count = lax.axis_size("wall")
    return lax.ppermute(value, "wall", [(i, i ^ bit) for i in range(count)])


def partner(value):
    count = lax.axis_size("span")
    return lax.ppermute(value, "span", [(i, i ^ 1) for i in range(count)])


def far(value, first):
    count = lax.axis_size("span")
    pairs = []
    for i in range(count):
        up = (i % 2 == 1) == first
        pairs.append((i, (i + (REACH if up else -REACH)) % count))
    return lax.ppermute(value, "span", pairs)


def params():
    return pltpu.CompilerParams(vmem_limit_bytes=20 << 20)


SMEM = pl.BlockSpec(memory_space=pltpu.SMEM)
VMEM = pl.BlockSpec(memory_space=pltpu.VMEM)


def split_kernel(width, x_ref, *out_refs):
    chunks = len(out_refs)
    cw = width // chunks
    half = cw // 2
    per = LANES // width
    lower = lax.broadcasted_iota(jnp.int32, (half, LANES), 1) < HALF

    def step(g, _):
        lows = []
        for u in range(2):
            lanes = pl.ds(pl.multiple_of((2 * g + u) * LANES, LANES), LANES)
            top = x_ref[:LANES, lanes].T.reshape(per, width, LANES)
            for k, out_ref in enumerate(out_refs):
                out_ref[pl.ds((2 * g + u) * per, per), :cw, :] = top[:, k * cw : (k + 1) * cw, :]
            lows.append(x_ref[LANES:, lanes])
        pair = jnp.concatenate(lows, 0).T
        for z in range(per):
            for k, out_ref in enumerate(out_refs):
                row = z * width + k * cw
                first, second = pair[row : row + half], pair[row + half : row + cw]
                out_ref[2 * g * per + z, cw:, :] = jnp.where(lower, first, pltpu.roll(second, HALF, 1))
                out_ref[(2 * g + 1) * per + z, cw:, :] = jnp.where(lower, pltpu.roll(first, HALF, 1), second)
        return 0

    lax.fori_loop(0, x_ref.shape[1] // (2 * LANES), step, 0, unroll=2)


def split(x, chunks, points):
    rows, breadth = x.shape
    width = breadth // points
    cw = width // chunks
    out = jax.ShapeDtypeStruct((points, cw + cw // 2, LANES), x.dtype)
    return pl.pallas_call(
        functools.partial(split_kernel, width),
        out_shape=(out,) * chunks,
        in_specs=[VMEM],
        out_specs=(VMEM,) * chunks,
        compiler_params=params(),
        cost_estimate=pl.CostEstimate(flops=0, bytes_accessed=8 * rows * breadth, transcendentals=0),
        name="split",
    )(x)


def join_top(width, parts, out_ref, begin, end):
    cw = width // len(parts)
    per = LANES // width
    for g in range(begin, end):
        rows = [part[g * per + z, :cw, :] for z in range(per) for part in parts]
        out_ref[:LANES, g * LANES : (g + 1) * LANES] = jnp.concatenate(rows, 0).T


def join_low(width, sol_parts, res_parts, sol_ref, res_ref, begin, end):
    cw = width // len(sol_parts)
    half = cw // 2
    per = LANES // width
    lower = lax.broadcasted_iota(jnp.int32, (half, LANES), 1) < HALF
    for g in range(begin, end):
        rows = []
        for z in range(per):
            for sol, res in zip(sol_parts, res_parts):
                a = sol[g * per + z, cw:, :]
                b = res[g * per + z, cw:, :]
                rows.append(jnp.where(lower, a, pltpu.roll(b, HALF, 1)))
                rows.append(jnp.where(lower, pltpu.roll(a, HALF, 1), b))
        both = jnp.concatenate(rows, 0).T
        lanes = slice(g * LANES, (g + 1) * LANES)
        sol_ref[LANES:, lanes] = both[:HALF]
        res_ref[LANES:, lanes] = both[HALF:]


def own_sign():
    return 1 - 2 * lax.rem(lax.axis_index("span"), 2)


def read(off_ref):
    value = off_ref[...]
    return [value[b, 0] for b in range(value.shape[0])]


UNROLL = 4


def fill(ext_ref, pieces):
    def step(i, _):
        here = pl.ds(i * 2 * UNROLL, 2 * UNROLL)
        ext_ref[here] = jnp.zeros((2 * UNROLL, *ext_ref.shape[1:]), jnp.float32)
        return 0

    lax.fori_loop(0, ext_ref.shape[0] // (2 * UNROLL), step, 0, unroll=2)
    place(ext_ref, pieces)


def place(ext_ref, pieces):
    for ref, at in pieces:

        def copy(i, _, ref=ref, at=at):
            ext_ref[pl.ds(at + i * UNROLL, UNROLL)] = ref[pl.ds(i * UNROLL, UNROLL)]
            return 0

        lax.fori_loop(0, ref.shape[0] // UNROLL, copy, 0)


def in_order(refs, at):
    out = []
    for ref in refs:
        out.append((ref, at))
        at = at + ref.shape[0]
    return out


def scaled(w_ref, row, value, cw):
    top = w_ref[0, pl.ds(row, 1), :] * value[:cw]
    low = w_ref[1, pl.ds(row, 1), :] * value[cw:]
    return top, low


def near_kernel(bands, off_ref, x_ref, w_ref, theirs_ref, *rest):
    *fars, partial_ref, sum_ref, ext_ref = rest
    points, rows, _ = x_ref.shape
    cw = rows * 2 // 3
    sign = own_sign()
    offsets = read(off_ref)
    own = jnp.where(sign > 0, REACH, REACH + 1)
    fill(ext_ref, [(x_ref, own * points), *in_order(fars, (own + 2 * sign) * points)])

    for out_ref, weights, shift in ((partial_ref, theirs_ref, sign), (sum_ref, w_ref, 0)):
        starts = [(own + shift) * points + offsets[b] for b in range(bands)]

        def step(i, _):
            for u in range(UNROLL):
                p = i * UNROLL + u
                if out_ref is sum_ref:
                    top, low = scaled(weights, bands * points + p, x_ref[p], cw)
                else:
                    top, low = None, None
                for b in range(bands):
                    t, l = scaled(weights, b * points + p, ext_ref[starts[b] + p], cw)
                    top, low = (t, l) if top is None else (top + t, low + l)
                out_ref[p, :cw, :] = top
                out_ref[p, cw:, :] = low
            return 0

        lax.fori_loop(0, points // UNROLL, step, 0)


def near(offsets, x, first, w, theirs):
    bands = offsets.shape[0]
    points, rows, _ = x.shape
    out = jax.ShapeDtypeStruct(x.shape, x.dtype)
    return pl.pallas_call(
        functools.partial(near_kernel, bands),
        out_shape=(out, out),
        in_specs=[VMEM] * (4 + len(first)),
        out_specs=(VMEM, VMEM),
        scratch_shapes=[pltpu.VMEM(((2 * REACH + 2) * points, rows, LANES), jnp.float32)],
        compiler_params=params(),
        cost_estimate=pl.CostEstimate(flops=1000000000, bytes_accessed=6 * x.size * 4, transcendentals=0),
        name="near",
    )(offsets, x, w, theirs, *first)


def halves(value):
    high = value.astype(jnp.bfloat16)
    low = (value - high.astype(jnp.float32)).astype(jnp.bfloat16)
    return high, low


def product(high, low, w_high, w_low):
    dot = functools.partial(jnp.dot, preferred_element_type=jnp.float32)
    return dot(high, w_high) + (dot(low, w_high) + dot(high, w_low))


def stage(high_ref, low_ref, at, ref, cw):
    points = ref.shape[0]
    half = cw // 2
    count = points * half
    low = ref[:, cw:, :].reshape(count, LANES)
    turned = pltpu.roll(low, HALF, 1)
    for part, top, rest in ((0, ref[:, :half, :], low), (1, ref[:, half:cw, :], turned)):
        rows = slice(part * count, (part + 1) * count)
        for n, value in enumerate((top.reshape(count, LANES), rest)):
            columns = slice(at + n * LANES, at + (n + 1) * LANES)
            high, small = halves(value)
            high_ref[rows, columns] = high
            low_ref[rows, columns] = small


def unstage(value, points, cw):
    half = cw // 2
    count = points * half
    first, second = value[:count], value[count:]
    top = [v[:, :LANES].reshape(points, half, LANES) for v in (first, second)]
    low = first[:, LANES:] + pltpu.roll(second[:, LANES:], HALF, 1)
    return top, low.reshape(points, half, LANES)


def wall_kernel(n_blocks, f_ref, s_ref, mh_ref, ml_ref, *rest):
    blocks = rest[:n_blocks]
    out_ref, high_ref, low_ref = rest[n_blocks:]
    points, rows, _ = f_ref.shape
    cw = rows * 2 // 3
    half = cw // 2
    for k, ref in enumerate(blocks):
        stage(high_ref, low_ref, 2 * LANES * k, ref, cw)
    result = product(high_ref[...], low_ref[...], mh_ref[...], ml_ref[...])
    top, low = unstage(result, points, cw)
    out_ref[:, :half, :] = f_ref[:, :half, :] - s_ref[:, :half, :] - top[0]
    out_ref[:, half:cw, :] = f_ref[:, half:cw, :] - s_ref[:, half:cw, :] - top[1]
    out_ref[:, cw:, :] = f_ref[:, cw:, :] - s_ref[:, cw:, :] - low


def wall(f, s, mh, ml, blocks):
    points, rows, _ = f.shape
    n_blocks = len(blocks)
    m_rows = points * rows * 2 // 3
    return pl.pallas_call(
        functools.partial(wall_kernel, n_blocks),
        out_shape=jax.ShapeDtypeStruct(f.shape, f.dtype),
        in_specs=[VMEM] * (4 + n_blocks),
        out_specs=VMEM,
        scratch_shapes=[pltpu.VMEM((m_rows, 2 * LANES * n_blocks), jnp.bfloat16)] * 2,
        compiler_params=params(),
        cost_estimate=pl.CostEstimate(flops=3000000000, bytes_accessed=8 * f.size * 4, transcendentals=0),
        name="wall",
    )(f, s, mh, ml, *blocks)


def far_terms(lo, n, off_ref, w_ref, far_ref, r_ref):
    points, rows, _ = far_ref.shape
    cw = rows * 2 // 3

    sign = own_sign()
    for b, offset in enumerate(read(off_ref)):
        shift = offset + 2 * sign * points
        first = jnp.maximum(lo, -shift)
        count = jnp.minimum(lo + n, points - shift) - first

        def point(p, b=b, shift=shift):
            top, low = scaled(w_ref, b * points + p, far_ref[p + shift], cw)
            r_ref[p - lo, :cw, :] = r_ref[p - lo, :cw, :] - top
            r_ref[p - lo, cw:, :] = r_ref[p - lo, cw:, :] - low

        def several(i, _, first=first, point=point):
            for u in range(UNROLL):
                point(first + i * UNROLL + u)
            return 0

        def one(i, _, first=first, point=point):
            point(first + i)
            return 0

        groups = jnp.maximum(count, 0) // UNROLL
        lax.fori_loop(0, groups, several, 0)
        lax.fori_loop(groups * UNROLL, count, one, 0)


def update(x_ref, lo, r_ref, high_ref, low_ref, bh_ref, bl_ref, x_new_ref):
    n, rows, _ = r_ref.shape
    cw = rows * 2 // 3
    half = cw // 2
    stage(high_ref, low_ref, 0, r_ref, cw)
    result = product(high_ref[...], low_ref[...], bh_ref[...], bl_ref[...])
    top, low = unstage(result, n, cw)
    here = pl.ds(lo, n)
    x_new_ref[:, :half, :] = x_ref[here, :half, :] + top[0]
    x_new_ref[:, half:cw, :] = x_ref[here, half:cw, :] + top[1]
    x_new_ref[:, cw:, :] = x_ref[here, cw:, :] + low


def last_kernel(off_ref, g_ref, t_ref, x_ref, w_ref, bh_ref, bl_ref, *rest):
    *fars, x_new_ref, r_ref, high_ref, low_ref, far_ref = rest
    points = x_ref.shape[0]
    if len(fars) > 1:
        place(far_ref, in_order(fars, 0))
    else:
        far_ref = fars[0]

    def begin(i, _):
        here = pl.ds(i * UNROLL, UNROLL)
        r_ref[here] = g_ref[here] - t_ref[here]
        return 0

    lax.fori_loop(0, points // UNROLL, begin, 0)
    far_terms(0, points, off_ref, w_ref, far_ref, r_ref)
    update(x_ref, 0, r_ref, high_ref, low_ref, bh_ref, bl_ref, x_new_ref)


def last(offsets, g, t, x, w, bh, bl, second):
    points, rows, _ = x.shape
    out = jax.ShapeDtypeStruct(x.shape, x.dtype)
    m_rows = points * rows * 2 // 3
    return pl.pallas_call(
        last_kernel,
        out_shape=(out, out),
        in_specs=[VMEM] * (7 + len(second)),
        out_specs=(VMEM, VMEM),
        scratch_shapes=[pltpu.VMEM((m_rows, 2 * LANES), jnp.bfloat16)] * 2
        + [pltpu.VMEM(x.shape if len(second) > 1 else (1, 8, LANES), jnp.float32)],
        compiler_params=params(),
        cost_estimate=pl.CostEstimate(flops=1000000000, bytes_accessed=8 * x.size * 4, transcendentals=0),
        name="last",
    )(offsets, g, t, x, w, bh, bl, *second)


def piece_start(sizes, i, points):
    before = sum(sizes[:i])
    even = lax.rem(lax.axis_index("span"), 2) == 0
    return jnp.where(even, points - before - sizes[i], before)


def finish_kernel(width, sizes, i, off_ref, g_ref, t_ref, x_ref, w_ref, bh_ref, bl_ref, *rest):
    fars = rest[: i + 1]
    n_outs = 2 if i else 0
    *earlier, sol_hbm, res_hbm, far_ref, high_ref, low_ref, x_new_ref, r_ref, sol_ref, res_ref, sems = rest[i + 1 :]
    if i:
        earlier = earlier[:-n_outs]
    points = x_ref.shape[0]
    n = sizes[i]
    lo = piece_start(sizes, i, points)
    place(far_ref, [(ref, piece_start(sizes, m, points)) for m, ref in enumerate(fars)])

    def begin(j, _):
        here = pl.ds(lo + j * UNROLL, UNROLL)
        r_ref[pl.ds(j * UNROLL, UNROLL)] = g_ref[here] - t_ref[here]
        return 0

    lax.fori_loop(0, n // UNROLL, begin, 0)
    far_terms(lo, n, off_ref, w_ref, far_ref, r_ref)
    views = [ref.at[pl.ds(lo, n)] for ref in earlier]
    sols, ress = [*views[::2], x_new_ref], [*views[1::2], r_ref]
    vectors = n * width // LANES
    join_top(width, ress, res_ref, 0, vectors)
    update(x_ref, lo, r_ref, high_ref, low_ref, bh_ref, bl_ref, x_new_ref)
    slabs = sems.shape[1]
    each = vectors // slabs
    copies = []
    for m in range(slabs):
        join_top(width, sols, sol_ref, m * each, (m + 1) * each)
        join_low(width, sols, ress, sol_ref, res_ref, m * each, (m + 1) * each)
        here = pl.ds(m * each * LANES, each * LANES)
        there = pl.ds(pl.multiple_of(lo * width + m * each * LANES, LANES), each * LANES)
        for which, (ref, hbm) in enumerate(((sol_ref, sol_hbm), (res_ref, res_hbm))):
            copy = pltpu.make_async_copy(ref.at[:, here], hbm.at[:, there], sems.at[which, m])
            copy.start()
            copies.append(copy)
    for copy in copies:
        copy.wait()


SLABS = 2


def finish(offsets, g, t, x, w, bh, bl, fars, earlier, outs, sizes, i, width):
    points, rows, _ = x.shape
    n = sizes[i]
    piece = pltpu.VMEM((n, rows, LANES), jnp.float32)
    out = jax.ShapeDtypeStruct((LANES + HALF, points * width), x.dtype)
    m_rows = n * rows * 2 // 3
    slab = pltpu.VMEM((LANES + HALF, n * width), jnp.float32)
    hbm = pl.BlockSpec(memory_space=pltpu.HBM)
    inputs = (offsets, g, t, x, w, bh, bl, *fars, *earlier)
    return pl.pallas_call(
        functools.partial(finish_kernel, width, sizes, i),
        out_shape=(out, out),
        in_specs=[VMEM] * len(inputs) + [hbm] * len(outs),
        out_specs=(hbm, hbm),
        input_output_aliases={len(inputs) + k: k for k in range(len(outs))},
        scratch_shapes=[
            pltpu.VMEM(x.shape, jnp.float32),
            pltpu.VMEM((m_rows, 2 * LANES), jnp.bfloat16),
            pltpu.VMEM((m_rows, 2 * LANES), jnp.bfloat16),
            piece,
            piece,
            slab,
            slab,
            pltpu.SemaphoreType.DMA((2, SLABS)),
        ],
        compiler_params=params(),
        cost_estimate=pl.CostEstimate(flops=1000000000, bytes_accessed=8 * x.size * 4, transcendentals=0),
        name="finish",
    )(*inputs, *outs)


def flip_matrix(rows, turned):
    size = 2 * LANES
    i = lax.broadcasted_iota(jnp.int32, (size, size), 0)
    j = lax.broadcasted_iota(jnp.int32, (size, size), 1)
    target = jnp.where(turned, rows - 1 - i, i)
    return jnp.where(jnp.logical_and(j == target, i < rows), 1.0, 0.0).astype(jnp.bfloat16)


def prep_kernel(count, index_ref, even_ref, odd_ref, inv_ref, mh_ref, ml_ref, bh_ref, bl_ref, pad_ref):
    rows = inv_ref.shape[0]
    size = 2 * LANES
    index = index_ref[0]
    half = count // 2
    lower = index >= half
    at = pl.ds(pl.multiple_of(jnp.where(lower, count - 1 - index, index) * rows, 8), rows)
    pad_ref[...] = jnp.zeros_like(pad_ref)

    def transposed(value):
        pad_ref[:rows, :rows] = value
        return pad_ref[...].T

    high, low = halves(transposed(inv_ref[...]))
    bh_ref[...] = high
    bl_ref[...] = low
    keep_or_turn = flip_matrix(rows, lower)
    turn = flip_matrix(rows, True)
    dot = functools.partial(jnp.dot, preferred_element_type=jnp.float32)
    even = even_ref[at, :]
    odd = odd_ref[at, :]
    for j in range(count):
        block = j if j < half else count - 1 - j
        columns = slice(block * rows, (block + 1) * rows)
        weight = jnp.where(lower == (j >= half), 0.5, -0.5)
        parts = halves(transposed(0.5 * even[:, columns] + weight * odd[:, columns]))
        place = pl.ds(pl.multiple_of(jnp.bitwise_xor(index, j) * size, size), size)
        for out_ref, part in zip((mh_ref, ml_ref), parts):
            if j >= half:
                part = dot(turn, part).astype(jnp.bfloat16)
            out_ref[place, :] = dot(part, keep_or_turn).astype(jnp.bfloat16)


def prep(wall_even, wall_odd, block_inv):
    count = lax.axis_size("wall")
    index = lax.axis_index("wall").astype(jnp.int32)[None]
    size = 2 * LANES
    m = jax.ShapeDtypeStruct((count * size, size), jnp.bfloat16)
    b = jax.ShapeDtypeStruct((size, size), jnp.bfloat16)
    return pl.pallas_call(
        functools.partial(prep_kernel, count),
        out_shape=(m, m, b, b),
        in_specs=[SMEM, VMEM, VMEM, VMEM],
        out_specs=(VMEM,) * 4,
        scratch_shapes=[pltpu.VMEM((size, size), jnp.float32)],
        compiler_params=params(),
        cost_estimate=pl.CostEstimate(flops=600000000, bytes_accessed=3000000, transcendentals=0),
        name="prep",
    )(index, wall_even, wall_odd, block_inv)


def after(value, *others):
    return lax.optimization_barrier((value, *others))[0]


def sweeps(forcing, start, wall_even, wall_odd, diag_shift, band_coef, offsets, pattern, block_inv):
    rows, breadth = start.shape
    points = diag_shift.shape[1]
    bands = band_coef.shape[0]
    width = breadth // points
    chunks = CHUNKS
    n_wall = lax.axis_size("wall")
    offsets = jnp.broadcast_to(offsets[:, None], (bands, LANES))

    raw_first = far(start, True)
    state = list(split(start, chunks, points))
    weights = jnp.swapaxes(band_coef, 1, 2) * pattern.astype(jnp.float32)[:, :, None]
    weights = jnp.concatenate([weights, diag_shift.T[None]], 0).reshape((bands + 1) * points, rows)
    low = weights[:, LANES:]
    own_w = jnp.stack([weights[:, :LANES], jnp.concatenate([low, low], 1)])
    their_w = partner(own_w[:, : bands * points])
    mh, ml, bh, bl = prep(wall_even, wall_odd, block_inv)
    f = split(forcing, chunks, points)
    sizes = (points * 5 // 8, points * 3 // 8)
    main = points - points // 8
    arrived = raw_first
    order = [0]
    bit = n_wall // 2
    while bit:
        order = order + [o ^ bit for o in order]
        bit //= 2
    for sweep in range(SWEEPS):
        final_sweep = sweep == SWEEPS - 1

        def move(k, first, arrived):
            value = after(state[k], arrived)
            if k < chunks - 1:
                parts = [value]
            elif final_sweep and not first:
                parts = [lax.dynamic_slice_in_dim(value, piece_start(sizes, i, points), n, 0) for i, n in enumerate(sizes)]
            else:
                parts = [value[:main], value[main:]]
            return [far(v, first) for v in parts]

        if sweep:
            firsts = [move(k, True, arrived) for k in range(chunks)]
            arrived = firsts[-1][0]
        else:
            firsts = [[v] for v in split(raw_first, chunks, points)]
        seconds = [move(k, False, arrived) for k in range(chunks)]
        arrived = seconds[-1][0]
        walls = []
        for k in range(chunks):
            got = [state[k]]
            bit = n_wall // 2
            while bit:
                got = got + [exchange(v, bit) for v in got]
                bit //= 2
            walls.append([got[order.index(o)] for o in range(n_wall)])
        theirs = []
        sums = []
        for k in range(chunks):
            partial, own_sum = near(offsets, state[k], firsts[k], own_w, their_w)
            sums.append(own_sum)
            theirs.append(partner(partial))
        new = []
        for k in range(chunks):
            g = wall(f[k], sums[k], mh, ml, walls[k])
            if final_sweep and k == chunks - 1:
                earlier = [a for pair in new for a in pair]
                outs = ()
                for i in range(len(sizes)):
                    call = functools.partial(finish, sizes=sizes, i=i, width=width)
                    fars = seconds[k][: i + 1]
                    outs = call(offsets, g, theirs[k], state[k], own_w, bh, bl, fars, earlier, outs)
                return outs
            new.append(last(offsets, g, theirs[k], state[k], own_w, bh, bl, seconds[k]))
        state = [pair[0] for pair in new]


def solution(mesh):
    in_specs = (
        P("wall", "span"),
        P("wall", "span"),
        P(),
        P(),
        P("wall", "span"),
        P(None, "wall", "span"),
        P(),
        P(None, "span"),
        P("wall", None),
    )
    out_specs = (P("wall", "span"), P("wall", "span"))
    return jax.shard_map(sweeps, mesh=mesh, in_specs=in_specs, out_specs=out_specs, check_vma=False)
```

```python
import functools

import jax
import jax.numpy as jnp
from jax import lax
from jax.experimental import pallas as pl
from jax.experimental.pallas import tpu as pltpu
from jax.sharding import PartitionSpec as P


SWEEPS = 2
CHUNKS = 2
LANES = 128
HALF = LANES // 2
REACH = 2


def exchange(value, bit):
    count = lax.axis_size("wall")
    return lax.ppermute(value, "wall", [(i, i ^ bit) for i in range(count)])


def partner(value):
    count = lax.axis_size("span")
    return lax.ppermute(value, "span", [(i, i ^ 1) for i in range(count)])


def far(value, first):
    count = lax.axis_size("span")
    pairs = []
    for i in range(count):
        up = (i % 2 == 1) == first
        pairs.append((i, (i + (REACH if up else -REACH)) % count))
    return lax.ppermute(value, "span", pairs)


def params():
    return pltpu.CompilerParams(vmem_limit_bytes=20 << 20)


SMEM = pl.BlockSpec(memory_space=pltpu.SMEM)
VMEM = pl.BlockSpec(memory_space=pltpu.VMEM)


def split_kernel(width, x_ref, *out_refs):
    chunks = len(out_refs)
    cw = width // chunks
    half = cw // 2
    per = LANES // width
    lower = lax.broadcasted_iota(jnp.int32, (half, LANES), 1) < HALF

    def step(g, _):
        lows = []
        for u in range(2):
            lanes = pl.ds(pl.multiple_of((2 * g + u) * LANES, LANES), LANES)
            top = x_ref[:LANES, lanes].T.reshape(per, width, LANES)
            for k, out_ref in enumerate(out_refs):
                out_ref[pl.ds((2 * g + u) * per, per), :cw, :] = top[:, k * cw : (k + 1) * cw, :]
            lows.append(x_ref[LANES:, lanes])
        pair = jnp.concatenate(lows, 0).T
        for z in range(per):
            for k, out_ref in enumerate(out_refs):
                row = z * width + k * cw
                first, second = pair[row : row + half], pair[row + half : row + cw]
                out_ref[2 * g * per + z, cw:, :] = jnp.where(lower, first, pltpu.roll(second, HALF, 1))
                out_ref[(2 * g + 1) * per + z, cw:, :] = jnp.where(lower, pltpu.roll(first, HALF, 1), second)
        return 0

    lax.fori_loop(0, x_ref.shape[1] // (2 * LANES), step, 0, unroll=2)


def split(x, chunks, points):
    rows, breadth = x.shape
    width = breadth // points
    cw = width // chunks
    out = jax.ShapeDtypeStruct((points, cw + cw // 2, LANES), x.dtype)
    return pl.pallas_call(
        functools.partial(split_kernel, width),
        out_shape=(out,) * chunks,
        in_specs=[VMEM],
        out_specs=(VMEM,) * chunks,
        compiler_params=params(),
        cost_estimate=pl.CostEstimate(flops=0, bytes_accessed=8 * rows * breadth, transcendentals=0),
        name="split",
    )(x)


def join_top(width, parts, out_ref, begin, end):
    cw = width // len(parts)
    per = LANES // width
    for g in range(begin, end):
        rows = [part[g * per + z, :cw, :] for z in range(per) for part in parts]
        out_ref[:LANES, g * LANES : (g + 1) * LANES] = jnp.concatenate(rows, 0).T


def join_low(width, sol_parts, res_parts, sol_ref, res_ref, begin, end):
    cw = width // len(sol_parts)
    half = cw // 2
    per = LANES // width
    lower = lax.broadcasted_iota(jnp.int32, (half, LANES), 1) < HALF
    for g in range(begin, end):
        rows = []
        for z in range(per):
            for sol, res in zip(sol_parts, res_parts):
                a = sol[g * per + z, cw:, :]
                b = res[g * per + z, cw:, :]
                rows.append(jnp.where(lower, a, pltpu.roll(b, HALF, 1)))
                rows.append(jnp.where(lower, pltpu.roll(a, HALF, 1), b))
        both = jnp.concatenate(rows, 0).T
        lanes = slice(g * LANES, (g + 1) * LANES)
        sol_ref[LANES:, lanes] = both[:HALF]
        res_ref[LANES:, lanes] = both[HALF:]


def own_sign():
    return 1 - 2 * lax.rem(lax.axis_index("span"), 2)


def read(off_ref):
    value = off_ref[...]
    return [value[b, 0] for b in range(value.shape[0])]


UNROLL = 4


def fill(ext_ref, pieces, points):
    def step(i, _):
        for slot in range(ext_ref.shape[0] // points):
            here = pl.ds(slot * points + i * UNROLL, UNROLL)
            ext_ref[here] = jnp.zeros((UNROLL, *ext_ref.shape[1:]), jnp.float32)
        return 0

    lax.fori_loop(0, points // UNROLL, step, 0)

    def copy(i, _):
        for ref, slot in pieces:
            ext_ref[pl.ds(slot * points + i * UNROLL, UNROLL)] = ref[pl.ds(i * UNROLL, UNROLL)]
        return 0

    lax.fori_loop(0, points // UNROLL, copy, 0)


def scaled(w_ref, row, value, cw):
    top = w_ref[0, pl.ds(row, 1), :] * value[:cw]
    low = w_ref[1, pl.ds(row, 1), :] * value[cw:]
    return top, low


def near_kernel(bands, off_ref, x_ref, far_ref, w_ref, theirs_ref, partial_ref, sum_ref, ext_ref):
    points, rows, _ = x_ref.shape
    cw = rows * 2 // 3
    sign = own_sign()
    offsets = read(off_ref)
    own = jnp.where(sign > 0, REACH, REACH + 1)
    fill(ext_ref, [(x_ref, own), (far_ref, own + 2 * sign)], points)

    for out_ref, weights, shift in ((partial_ref, theirs_ref, sign), (sum_ref, w_ref, 0)):
        starts = [(own + shift) * points + offsets[b] for b in range(bands)]

        def step(i, _):
            for u in range(UNROLL):
                p = i * UNROLL + u
                if out_ref is sum_ref:
                    top, low = scaled(weights, bands * points + p, x_ref[p], cw)
                else:
                    top, low = None, None
                for b in range(bands):
                    t, l = scaled(weights, b * points + p, ext_ref[starts[b] + p], cw)
                    top, low = (t, l) if top is None else (top + t, low + l)
                out_ref[p, :cw, :] = top
                out_ref[p, cw:, :] = low
            return 0

        lax.fori_loop(0, points // UNROLL, step, 0)


def near(offsets, x, first, w, theirs):
    bands = offsets.shape[0]
    points, rows, _ = x.shape
    out = jax.ShapeDtypeStruct(x.shape, x.dtype)
    return pl.pallas_call(
        functools.partial(near_kernel, bands),
        out_shape=(out, out),
        in_specs=[VMEM] * 5,
        out_specs=(VMEM, VMEM),
        scratch_shapes=[pltpu.VMEM(((2 * REACH + 2) * points, rows, LANES), jnp.float32)],
        compiler_params=params(),
        cost_estimate=pl.CostEstimate(flops=1000000000, bytes_accessed=6 * x.size * 4, transcendentals=0),
        name="near",
    )(offsets, x, first, w, theirs)


def halves(value):
    high = value.astype(jnp.bfloat16)
    low = (value - high.astype(jnp.float32)).astype(jnp.bfloat16)
    return high, low


def product(high, low, w_high, w_low):
    dot = functools.partial(jnp.dot, preferred_element_type=jnp.float32)
    return dot(high, w_high) + (dot(low, w_high) + dot(high, w_low))


def stage(high_ref, low_ref, at, ref, cw):
    points = ref.shape[0]
    half = cw // 2
    count = points * half
    low = ref[:, cw:, :].reshape(count, LANES)
    turned = pltpu.roll(low, HALF, 1)
    for part, top, rest in ((0, ref[:, :half, :], low), (1, ref[:, half:cw, :], turned)):
        rows = slice(part * count, (part + 1) * count)
        for n, value in enumerate((top.reshape(count, LANES), rest)):
            columns = slice(at + n * LANES, at + (n + 1) * LANES)
            high, small = halves(value)
            high_ref[rows, columns] = high
            low_ref[rows, columns] = small


def unstage(value, points, cw):
    half = cw // 2
    count = points * half
    first, second = value[:count], value[count:]
    top = [v[:, :LANES].reshape(points, half, LANES) for v in (first, second)]
    low = first[:, LANES:] + pltpu.roll(second[:, LANES:], HALF, 1)
    return top, low.reshape(points, half, LANES)


def wall_kernel(n_blocks, f_ref, s_ref, mh_ref, ml_ref, *rest):
    blocks = rest[:n_blocks]
    out_ref, high_ref, low_ref = rest[n_blocks:]
    points, rows, _ = f_ref.shape
    cw = rows * 2 // 3
    half = cw // 2
    for k, ref in enumerate(blocks):
        stage(high_ref, low_ref, 2 * LANES * k, ref, cw)
    result = product(high_ref[...], low_ref[...], mh_ref[...], ml_ref[...])
    top, low = unstage(result, points, cw)
    out_ref[:, :half, :] = f_ref[:, :half, :] - s_ref[:, :half, :] - top[0]
    out_ref[:, half:cw, :] = f_ref[:, half:cw, :] - s_ref[:, half:cw, :] - top[1]
    out_ref[:, cw:, :] = f_ref[:, cw:, :] - s_ref[:, cw:, :] - low


def wall(f, s, mh, ml, blocks):
    points, rows, _ = f.shape
    n_blocks = len(blocks)
    m_rows = points * rows * 2 // 3
    return pl.pallas_call(
        functools.partial(wall_kernel, n_blocks),
        out_shape=jax.ShapeDtypeStruct(f.shape, f.dtype),
        in_specs=[VMEM] * (4 + n_blocks),
        out_specs=VMEM,
        scratch_shapes=[pltpu.VMEM((m_rows, 2 * LANES * n_blocks), jnp.bfloat16)] * 2,
        compiler_params=params(),
        cost_estimate=pl.CostEstimate(flops=3000000000, bytes_accessed=8 * f.size * 4, transcendentals=0),
        name="wall",
    )(f, s, mh, ml, *blocks)


def far_terms(lo, n, points, base, off_ref, w_ref, far_ref, r_ref):
    rows = far_ref.shape[1]
    cw = rows * 2 // 3

    sign = own_sign()
    for b, offset in enumerate(read(off_ref)):
        shift = offset + 2 * sign * points
        first = jnp.maximum(lo, -shift)
        count = jnp.minimum(lo + n, points - shift) - first

        def point(p, b=b, shift=shift):
            top, low = scaled(w_ref, b * points + p, far_ref[p + shift - base], cw)
            r_ref[p - lo, :cw, :] = r_ref[p - lo, :cw, :] - top
            r_ref[p - lo, cw:, :] = r_ref[p - lo, cw:, :] - low

        def several(i, _, first=first, point=point):
            for u in range(UNROLL):
                point(first + i * UNROLL + u)
            return 0

        def one(i, _, first=first, point=point):
            point(first + i)
            return 0

        groups = jnp.maximum(count, 0) // UNROLL
        lax.fori_loop(0, groups, several, 0)
        lax.fori_loop(groups * UNROLL, count, one, 0)


def update(x_ref, lo, r_ref, high_ref, low_ref, bh_ref, bl_ref, x_new_ref):
    n, rows, _ = r_ref.shape
    cw = rows * 2 // 3
    half = cw // 2
    stage(high_ref, low_ref, 0, r_ref, cw)
    result = product(high_ref[...], low_ref[...], bh_ref[...], bl_ref[...])
    top, low = unstage(result, n, cw)
    here = pl.ds(lo, n)
    x_new_ref[:, :half, :] = x_ref[here, :half, :] + top[0]
    x_new_ref[:, half:cw, :] = x_ref[here, half:cw, :] + top[1]
    x_new_ref[:, cw:, :] = x_ref[here, cw:, :] + low


def last_kernel(off_ref, g_ref, t_ref, x_ref, w_ref, bh_ref, bl_ref, far_ref, x_new_ref, r_ref, high_ref, low_ref):
    points = x_ref.shape[0]

    def begin(i, _):
        here = pl.ds(i * UNROLL, UNROLL)
        r_ref[here] = g_ref[here] - t_ref[here]
        return 0

    lax.fori_loop(0, points // UNROLL, begin, 0)
    far_terms(0, points, points, 0, off_ref, w_ref, far_ref, r_ref)
    update(x_ref, 0, r_ref, high_ref, low_ref, bh_ref, bl_ref, x_new_ref)


def last(offsets, g, t, x, w, bh, bl, second):
    points, rows, _ = x.shape
    out = jax.ShapeDtypeStruct(x.shape, x.dtype)
    m_rows = points * rows * 2 // 3
    return pl.pallas_call(
        last_kernel,
        out_shape=(out, out),
        in_specs=[VMEM] * 8,
        out_specs=(VMEM, VMEM),
        scratch_shapes=[pltpu.VMEM((m_rows, 2 * LANES), jnp.bfloat16)] * 2,
        compiler_params=params(),
        cost_estimate=pl.CostEstimate(flops=1000000000, bytes_accessed=8 * x.size * 4, transcendentals=0),
        name="last",
    )(offsets, g, t, x, w, bh, bl, second)


def piece_start(sizes, i, points):
    before = sum(sizes[:i])
    even = lax.rem(lax.axis_index("span"), 2) == 0
    return jnp.where(even, points - before - sizes[i], before)


def finish_kernel(width, sizes, i, off_ref, g_ref, t_ref, x_ref, w_ref, bh_ref, bl_ref, *rest):
    fars = rest[: i + 1]
    n_outs = 2 if i else 0
    *earlier, sol_hbm, res_hbm, far_ref, high_ref, low_ref, x_new_ref, r_ref, sol_ref, res_ref, sems = rest[i + 1 :]
    if i:
        earlier = earlier[:-n_outs]
    points = x_ref.shape[0]
    n = sizes[i]
    lo = piece_start(sizes, i, points)
    base = 0
    if i == 0:
        far_ref, base = fars[0], lo
    else:
        for m, ref in enumerate(fars):
            at = piece_start(sizes, m, points)

            def copy(j, _, ref=ref, at=at):
                far_ref[pl.ds(at + j * UNROLL, UNROLL)] = ref[pl.ds(j * UNROLL, UNROLL)]
                return 0

            lax.fori_loop(0, sizes[m] // UNROLL, copy, 0, unroll=2)

    def begin(j, _):
        here = pl.ds(lo + j * UNROLL, UNROLL)
        r_ref[pl.ds(j * UNROLL, UNROLL)] = g_ref[here] - t_ref[here]
        return 0

    lax.fori_loop(0, n // UNROLL, begin, 0, unroll=2)
    far_terms(lo, n, points, base, off_ref, w_ref, far_ref, r_ref)
    views = [ref.at[pl.ds(lo, n)] for ref in earlier]
    sols, ress = [*views[::2], x_new_ref], [*views[1::2], r_ref]
    vectors = n * width // LANES
    join_top(width, ress, res_ref, 0, vectors)
    update(x_ref, lo, r_ref, high_ref, low_ref, bh_ref, bl_ref, x_new_ref)
    slabs = sems.shape[1]
    each = vectors // slabs
    copies = []
    for m in range(slabs):
        join_top(width, sols, sol_ref, m * each, (m + 1) * each)
        join_low(width, sols, ress, sol_ref, res_ref, m * each, (m + 1) * each)
        here = pl.ds(m * each * LANES, each * LANES)
        there = pl.ds(pl.multiple_of(lo * width + m * each * LANES, LANES), each * LANES)
        for which, (ref, hbm) in enumerate(((sol_ref, sol_hbm), (res_ref, res_hbm))):
            copy = pltpu.make_async_copy(ref.at[:, here], hbm.at[:, there], sems.at[which, m])
            copy.start()
            copies.append(copy)
    for copy in copies:
        copy.wait()


SLABS = 2


def finish(offsets, g, t, x, w, bh, bl, fars, earlier, outs, sizes, i, width):
    points, rows, _ = x.shape
    n = sizes[i]
    piece = pltpu.VMEM((n, rows, LANES), jnp.float32)
    out = jax.ShapeDtypeStruct((LANES + HALF, points * width), x.dtype)
    m_rows = n * rows * 2 // 3
    slab = pltpu.VMEM((LANES + HALF, n * width), jnp.float32)
    hbm = pl.BlockSpec(memory_space=pltpu.HBM)
    inputs = (offsets, g, t, x, w, bh, bl, *fars, *earlier)
    return pl.pallas_call(
        functools.partial(finish_kernel, width, sizes, i),
        out_shape=(out, out),
        in_specs=[VMEM] * len(inputs) + [hbm] * len(outs),
        out_specs=(hbm, hbm),
        input_output_aliases={len(inputs) + k: k for k in range(len(outs))},
        scratch_shapes=[
            pltpu.VMEM(x.shape, jnp.float32),
            pltpu.VMEM((m_rows, 2 * LANES), jnp.bfloat16),
            pltpu.VMEM((m_rows, 2 * LANES), jnp.bfloat16),
            piece,
            piece,
            slab,
            slab,
            pltpu.SemaphoreType.DMA((2, SLABS)),
        ],
        compiler_params=params(),
        cost_estimate=pl.CostEstimate(flops=1000000000, bytes_accessed=8 * x.size * 4, transcendentals=0),
        name="finish",
    )(*inputs, *outs)


def flip_matrix(rows, turned):
    size = 2 * LANES
    i = lax.broadcasted_iota(jnp.int32, (size, size), 0)
    j = lax.broadcasted_iota(jnp.int32, (size, size), 1)
    target = jnp.where(turned, rows - 1 - i, i)
    return jnp.where(jnp.logical_and(j == target, i < rows), 1.0, 0.0).astype(jnp.bfloat16)


def prep_kernel(count, index_ref, even_ref, odd_ref, inv_ref, mh_ref, ml_ref, bh_ref, bl_ref, pad_ref):
    rows = inv_ref.shape[0]
    size = 2 * LANES
    index = index_ref[0]
    half = count // 2
    lower = index >= half
    at = pl.ds(pl.multiple_of(jnp.where(lower, count - 1 - index, index) * rows, 8), rows)
    pad_ref[...] = jnp.zeros_like(pad_ref)

    def transposed(value):
        pad_ref[:rows, :rows] = value
        return pad_ref[...].T

    high, low = halves(transposed(inv_ref[...]))
    bh_ref[...] = high
    bl_ref[...] = low
    keep_or_turn = flip_matrix(rows, lower)
    turn = flip_matrix(rows, True)
    dot = functools.partial(jnp.dot, preferred_element_type=jnp.float32)
    even = even_ref[at, :]
    odd = odd_ref[at, :]
    for j in range(count):
        block = j if j < half else count - 1 - j
        columns = slice(block * rows, (block + 1) * rows)
        weight = jnp.where(lower == (j >= half), 0.5, -0.5)
        parts = halves(transposed(0.5 * even[:, columns] + weight * odd[:, columns]))
        place = pl.ds(pl.multiple_of(jnp.bitwise_xor(index, j) * size, size), size)
        for out_ref, part in zip((mh_ref, ml_ref), parts):
            if j >= half:
                part = dot(turn, part).astype(jnp.bfloat16)
            out_ref[place, :] = dot(part, keep_or_turn).astype(jnp.bfloat16)


def prep(wall_even, wall_odd, block_inv):
    count = lax.axis_size("wall")
    index = lax.axis_index("wall").astype(jnp.int32)[None]
    size = 2 * LANES
    m = jax.ShapeDtypeStruct((count * size, size), jnp.bfloat16)
    b = jax.ShapeDtypeStruct((size, size), jnp.bfloat16)
    return pl.pallas_call(
        functools.partial(prep_kernel, count),
        out_shape=(m, m, b, b),
        in_specs=[SMEM, VMEM, VMEM, VMEM],
        out_specs=(VMEM,) * 4,
        scratch_shapes=[pltpu.VMEM((size, size), jnp.float32)],
        compiler_params=params(),
        cost_estimate=pl.CostEstimate(flops=600000000, bytes_accessed=3000000, transcendentals=0),
        name="prep",
    )(index, wall_even, wall_odd, block_inv)


def after(value, *others):
    return lax.optimization_barrier((value, *others))[0]


def sweeps(forcing, start, wall_even, wall_odd, diag_shift, band_coef, offsets, pattern, block_inv):
    rows, breadth = start.shape
    points = diag_shift.shape[1]
    bands = band_coef.shape[0]
    width = breadth // points
    chunks = CHUNKS
    n_wall = lax.axis_size("wall")
    offsets = jnp.broadcast_to(offsets[:, None], (bands, LANES))

    raw_first = far(start, True)
    state = list(split(start, chunks, points))
    weights = jnp.swapaxes(band_coef, 1, 2) * pattern.astype(jnp.float32)[:, :, None]
    weights = jnp.concatenate([weights, diag_shift.T[None]], 0).reshape((bands + 1) * points, rows)
    low = weights[:, LANES:]
    own_w = jnp.stack([weights[:, :LANES], jnp.concatenate([low, low], 1)])
    their_w = partner(own_w[:, : bands * points])
    mh, ml, bh, bl = prep(wall_even, wall_odd, block_inv)
    f = split(forcing, chunks, points)
    sizes = (points * 3 // 8, points * 3 // 8, points // 4)
    arrived = raw_first
    order = [0]
    bit = n_wall // 2
    while bit:
        order = order + [o ^ bit for o in order]
        bit //= 2
    for sweep in range(SWEEPS):
        final_sweep = sweep == SWEEPS - 1
        if sweep:
            firsts = [far(after(state[k], arrived), True) for k in range(chunks)]
            arrived = firsts[-1]
        else:
            firsts = split(raw_first, chunks, points)
        seconds = []
        for k in range(chunks):
            value = after(state[k], arrived)
            if final_sweep and k == chunks - 1:
                parts = [lax.dynamic_slice_in_dim(value, piece_start(sizes, i, points), n, 0) for i, n in enumerate(sizes)]
                seconds.append([far(v, False) for v in parts])
            else:
                seconds.append(far(value, False))
        arrived = seconds[-1]
        walls = []
        for k in range(chunks):
            got = [state[k]]
            bit = n_wall // 2
            while bit:
                got = got + [exchange(v, bit) for v in got]
                bit //= 2
            walls.append([got[order.index(o)] for o in range(n_wall)])
        theirs = []
        sums = []
        for k in range(chunks):
            partial, own_sum = near(offsets, state[k], firsts[k], own_w, their_w)
            sums.append(own_sum)
            theirs.append(partner(partial))
        new = []
        for k in range(chunks):
            g = wall(f[k], sums[k], mh, ml, walls[k])
            if final_sweep and k == chunks - 1:
                earlier = [a for pair in new for a in pair]
                outs = ()
                for i in range(len(sizes)):
                    call = functools.partial(finish, sizes=sizes, i=i, width=width)
                    fars = seconds[k][: i + 1]
                    outs = call(offsets, g, theirs[k], state[k], own_w, bh, bl, fars, earlier, outs)
                return outs
            new.append(last(offsets, g, theirs[k], state[k], own_w, bh, bl, seconds[k]))
        state = [pair[0] for pair in new]


def solution(mesh):
    in_specs = (
        P("wall", "span"),
        P("wall", "span"),
        P(),
        P(),
        P("wall", "span"),
        P(None, "wall", "span"),
        P(),
        P(None, "span"),
        P("wall", None),
    )
    out_specs = (P("wall", "span"), P("wall", "span"))
    return jax.shard_map(sweeps, mesh=mesh, in_specs=in_specs, out_specs=out_specs, check_vma=False)
```
